128 devices in a mesh: seq: 8 (over y_lo, x), samp: 16 (over y_hi, z, core).
Axes of the slice: x: 4, y: 4 (y_hi: 2, y_lo: 2; y = y_hi * 2 + y_lo), z: 4, core: 2. Of those that a mesh axis runs over, the one named last changes fastest.
Arguments:
- prompt_ids: int32 [2048], replicated, may hold values from 0 to 64127
- comp_ids: int32 [64, 2], replicated, may hold values from 0 to 64127
- prefix_len: int32 [1], replicated, may hold values from 8192 to 16384
- prompt_offset: int32 [1], replicated, may hold values from 16384 to 32768
- embed_table: bfloat16 [64128, 8192], P('seq', 'samp'), may hold values from -3 to 3
- attn_gain: bfloat16 [8192], P('samp'), may hold values from 0.099609375 to 1.8984375
- query_key_value_weight: bfloat16 [8192, 10240], P('samp', 'seq')
- w_out: bfloat16 [8192, 8192], P('seq', 'samp'), may hold values from -0.29882812 to 0.29882812
- key_value_cache: bfloat16 [2, 8, 16384, 128], P(None, 'seq'), may hold values from -6 to 6
Outputs:
- prompt_out: bfloat16 [2048, 8192], P('seq', 'samp')
- comp_out: bfloat16 [64, 2, 8192], P('seq', None, 'samp')
The draws below stay inside these ranges and needn't reach their ends.
Inputs may be any that keep to these rules, and one draw needn't show every extreme that they name: The valid cache slots are slots 0 to prefix_len - 1. The valid cache slots hold the positions directly before prompt_offset.
All inputs are finite; a program needn't handle non-finite values.
Results may differ from the reference program's by a relative error of at most 0.03.
Values may be sent and summed in bfloat16 or wider, within the bound.
No kernel may reach another device: no remote copies, remote signals or barrier semaphores. Data moves between devices by JAX's collectives and lax.ppermute only.
A program may use at most 192 MiB of HBM per device.

```python
import math
import jax
import jax.numpy as jnp
import numpy as np
from jax import lax

MODEL_WIDTH = 8192
HQ = 64
KEY_HEADS = 8
HEAD_SIZE = 128
QUERY_PER_KEY = 8
VOCAB = 64128
NEW = 2
PREFIX_SLOTS = 16384
PROMPT = 2048
NCOMP = 64
N_SAMP = 16


def draw_query_key_value_weight(key, part):
    key_starting = jax.random.fold_in(key, 11)
    key_factor = jax.random.fold_in(key, 12)
    initial_sample = jax.random.normal(key_starting, (MODEL_WIDTH, KEY_HEADS, QUERY_PER_KEY + 2, HEAD_SIZE), jnp.float32)
    head_factor = jnp.exp(jax.random.uniform(key_factor, (1, KEY_HEADS, QUERY_PER_KEY, 1), jnp.float32, math.log(1.2), math.log(3.0)))
    query_part = initial_sample[:, :, :QUERY_PER_KEY] * head_factor
    paired = initial_sample[:, :, QUERY_PER_KEY:]
    combined_rows = jnp.concatenate([query_part, paired], axis=2) * (1.0 / math.sqrt(MODEL_WIDTH))
    return combined_rows.reshape(MODEL_WIDTH, KEY_HEADS * (QUERY_PER_KEY + 2) * HEAD_SIZE).astype(jnp.bfloat16)


def plant(result, own_key, least, largest):
    index_at = [jax.random.randint(jax.random.fold_in(own_key, axis), (), 0, length) for axis, length in enumerate(result.shape)]
    main_axis = result.shape.index(max(result.shape))
    beside = index_at[:main_axis] + [(index_at[main_axis] + 1) % result.shape[main_axis]] + index_at[main_axis + 1:]
    return result.at[tuple(index_at)].set(least).at[tuple(beside)].set(largest)


def levels(stream_key, shape, split, low, largest):
    factor_of, own = 1.0, jax.random.fold_in(stream_key, 6)
    for dim, parts in split:
        steps = jnp.exp(jax.random.uniform(jax.random.fold_in(own, dim), (parts,), jnp.float32, low / len(split), largest / len(split)))
        factor_of = factor_of * jnp.repeat(steps, shape[dim] // parts).reshape([-1 if axis == dim else 1 for axis in range(len(shape))])
    return factor_of


def cumulative_ranks(count, skew):
    portions = [(1 << 20) // math.isqrt(standing ** skew) + 1 for standing in range(1, count + 1)]
    spread = 1 + sum(portions) // (1 << 30)
    return np.cumsum(np.array([max(1, weight // spread) for weight in portions]))


def skewed_ids(key, shape, amount, slope):
    listing = cumulative_ranks(amount, slope)
    pick = jax.random.randint(jax.random.fold_in(key, 1), shape, 0, int(listing[amount - 1]))
    standing = jnp.searchsorted(jnp.asarray(listing, jnp.int32), pick, side="right")
    return jax.random.permutation(jax.random.fold_in(key, 2), amount)[standing].astype(jnp.int32)


def centred(rng, shape, width, limit, pieces=(), kind=jnp.bfloat16):
    result = width * jax.random.normal(rng, shape, jnp.float32)
    if pieces:
        result = result * levels(rng, shape, pieces, -0.22, 0.18)
    return jnp.clip(result, -limit, limit).astype(kind)


def setup_inputs(seed: int = 0) -> dict:
    streams_of = jax.random.split(jax.random.key(seed), 10)
    prompt_ids = plant(skewed_ids(streams_of[0], (PROMPT,), VOCAB, 2), jax.random.fold_in(streams_of[0], 3), 0, VOCAB - 1).astype(jnp.int32)
    comp_ids = plant(skewed_ids(streams_of[1], (NCOMP, NEW), VOCAB, 2), jax.random.fold_in(streams_of[1], 3), 0, VOCAB - 1).astype(jnp.int32)
    prefix_len = jax.random.randint(streams_of[2], (1,), PREFIX_SLOTS // 2, PREFIX_SLOTS + 1).astype(jnp.int32)
    prompt_offset = jax.random.randint(streams_of[3], (1,), PREFIX_SLOTS, 2 * PREFIX_SLOTS + 1).astype(jnp.int32)
    embed_table = centred(streams_of[4], (VOCAB, MODEL_WIDTH), 0.5, 3.0, ((0, 8), (1, 16)))
    attn_gain = jnp.clip(1.0 + 0.18 * jax.random.normal(streams_of[5], (MODEL_WIDTH,), jnp.float32), 0.099609375, 1.8984375).astype(jnp.bfloat16)
    query_key_value_weight = draw_query_key_value_weight(jax.random.fold_in(streams_of[9], 71), 0)
    w_out = centred(streams_of[7], (HQ * HEAD_SIZE, MODEL_WIDTH), 0.05, 0.29882812, ((0, 8), (1, 16)))
    key_value_cache = centred(streams_of[8], (2, KEY_HEADS, PREFIX_SLOTS, HEAD_SIZE), 1.0, 6.0, ((1, 8),))
    return dict(prompt_ids=prompt_ids, comp_ids=comp_ids, prefix_len=prefix_len, prompt_offset=prompt_offset, embed_table=embed_table, attn_gain=attn_gain, query_key_value_weight=query_key_value_weight, w_out=w_out, key_value_cache=key_value_cache)


NORM_EPS = 1e-05
MASK_FILL = -1e+30

def rope_freqs(head_dim):
    half_dim = head_dim // 2
    dim_index = jnp.arange(half_dim, dtype=jnp.float32)
    base_freq = 1.0 / jnp.power(500000.0, 2.0 * dim_index / head_dim)
    wavelength = 2.0 * math.pi / base_freq
    blend = (8192.0 / wavelength - 1.0) / 3.0
    middle = (1.0 - blend) * base_freq / 8.0 + blend * base_freq
    return jnp.where(wavelength > 8192.0, base_freq / 8.0, jnp.where(wavelength < 2048.0, base_freq, middle))

def rotate(vectors, positions):
    angles = positions[:, None] * rope_freqs(vectors.shape[-1])[None, :]
    bcast_shape = (angles.shape[0],) + (1,) * (vectors.ndim - 2) + (angles.shape[1],)
    cosine = jnp.cos(angles).reshape(bcast_shape)
    sine_vals = jnp.sin(angles).reshape(bcast_shape)
    half_dim = vectors.shape[-1] // 2
    first_half = vectors[..., :half_dim]
    second_half = vectors[..., half_dim:]
    return jnp.concatenate([first_half * cosine - second_half * sine_vals, second_half * cosine + first_half * sine_vals], axis=-1)

def attend_group(group_queries, cache_keys, cache_values, prompt_keys, prompt_values, comp_keys, comp_values, prefix_count):
    key_all = jnp.concatenate([cache_keys, prompt_keys, comp_keys], axis=0).astype(jnp.float32)
    value_all = jnp.concatenate([cache_values, prompt_values, comp_values], axis=0).astype(jnp.float32)
    row_overall_sum = group_queries.shape[0]
    block_rows = row_overall_sum // N_SAMP
    head_dim = group_queries.shape[-1]
    score_scale = 1.0 / math.sqrt(head_dim)
    slots = jnp.arange(PREFIX_SLOTS, dtype=jnp.int32)
    prompt_pos = jnp.arange(PROMPT, dtype=jnp.int32)
    comp_index = jnp.arange(NCOMP * NEW, dtype=jnp.int32)

    def block_attend(packed):
        query_block, row_index = packed
        scores = jnp.einsum('rqd,kd->rqk', query_block.astype(jnp.float32), key_all) * score_scale
        cache_live = jnp.broadcast_to((slots < prefix_count)[None, :], (row_index.shape[0], PREFIX_SLOTS))
        prompt_live = prompt_pos[None, :] <= row_index[:, None]
        comp_row = row_index - PROMPT
        comp_live = (row_index[:, None] >= PROMPT) & (comp_index[None, :] // NEW == comp_row[:, None] // NEW) & (comp_index[None, :] % NEW <= comp_row[:, None] % NEW)
        live_mask = jnp.concatenate([cache_live, prompt_live, comp_live], axis=1)[:, None, :]
        scores = jnp.where(live_mask, scores, MASK_FILL)
        peak = lax.optimization_barrier(jnp.max(scores, axis=-1, keepdims=True))
        weights = jnp.where(live_mask, jnp.exp(scores - peak), 0.0)
        weight_sum = lax.optimization_barrier(jnp.sum(weights, axis=-1, keepdims=True))
        rounded = lax.optimization_barrier(weights.astype(jnp.bfloat16)).astype(jnp.float32)
        context = jnp.einsum('rqk,kd->rqd', rounded, value_all) / weight_sum
        return context.astype(jnp.bfloat16)
    query_blocks = group_queries.reshape(N_SAMP, block_rows, QUERY_PER_KEY, head_dim)
    row_blocks = jnp.arange(row_overall_sum, dtype=jnp.int32).reshape(N_SAMP, block_rows)
    return lax.map(block_attend, (query_blocks, row_blocks)).reshape(row_overall_sum, QUERY_PER_KEY, head_dim)

def reference(prompt_ids, comp_ids, prefix_len, prompt_offset, embed_table, attn_gain, query_key_value_weight, w_out, key_value_cache):
    token_ids = jnp.concatenate([prompt_ids, comp_ids.reshape(-1)]).astype(jnp.int32)
    row_overall_sum = token_ids.shape[0]
    embedded = jnp.take(embed_table, token_ids, axis=0)
    wide = embedded.astype(jnp.float32)
    mean_square = lax.optimization_barrier(jnp.mean(wide * wide, axis=1, keepdims=True))
    normalized_rows = (wide * lax.rsqrt(mean_square + NORM_EPS) * attn_gain.astype(jnp.float32)[None, :]).astype(jnp.bfloat16)
    projected_rows = jnp.dot(normalized_rows, query_key_value_weight, preferred_element_type=jnp.float32).reshape(row_overall_sum, KEY_HEADS, QUERY_PER_KEY + 2, HEAD_SIZE)
    start_pos = prompt_offset[0]
    prompt_pos = start_pos + jnp.arange(PROMPT, dtype=jnp.int32)
    comp_pos = start_pos + PROMPT + jnp.arange(NCOMP * NEW, dtype=jnp.int32) % NEW
    positions = jnp.concatenate([prompt_pos, comp_pos]).astype(jnp.float32)
    queries = rotate(projected_rows[:, :, :QUERY_PER_KEY], positions).astype(jnp.bfloat16)
    key_rows = rotate(projected_rows[:, :, QUERY_PER_KEY], positions).astype(jnp.bfloat16)
    value_rows = projected_rows[:, :, QUERY_PER_KEY + 1].astype(jnp.bfloat16)
    prefix_count = prefix_len[0]

    def per_group(packed):
        group_queries, group_keys, group_values, cache_keys, cache_values = packed
        return attend_group(group_queries, cache_keys, cache_values, group_keys[:PROMPT], group_values[:PROMPT], group_keys[PROMPT:], group_values[PROMPT:], prefix_count)
    context = lax.map(per_group, (jnp.transpose(queries, (1, 0, 2, 3)), jnp.transpose(key_rows, (1, 0, 2)), jnp.transpose(value_rows, (1, 0, 2)), key_value_cache[0], key_value_cache[1]))
    context = jnp.transpose(context, (1, 0, 2, 3)).reshape(row_overall_sum, HQ * HEAD_SIZE)
    layer_out = (jnp.dot(context, w_out, preferred_element_type=jnp.float32) + wide).astype(jnp.bfloat16)
    return (layer_out[:PROMPT], layer_out[PROMPT:].reshape(NCOMP, NEW, MODEL_WIDTH))
```

```python
import functools
import math

import jax
import jax.numpy as jnp
from jax import lax
from jax.experimental import pallas as pl
from jax.experimental.pallas import tpu as pltpu
from jax.sharding import PartitionSpec as P


NORM_EPS = 1e-05
MASK_FILL = -1e30
HEAD = 128
HEADS = 8
SEQ = 8
GROUPS = 8
ROWS = 136
PROMPT_ROWS = 128
FEATURES = 8192
LOG2_SCALE = math.log2(math.e) / math.sqrt(HEAD)
LAST_DIMS = (((1,), (1,)), ((), ()))
COMP_ID = 1 << 20

SHIFTS = ((0, 0), (2, 1), (2, 0), (1, 1), (3, 1), (0, 1), (1, 0), (3, 0))


def rope_freqs(head_dim):
    half_dim = head_dim // 2
    dim_index = jnp.arange(half_dim, dtype=jnp.float32)
    base_freq = 1.0 / jnp.power(500000.0, 2.0 * dim_index / head_dim)
    wavelength = 2.0 * math.pi / base_freq
    blend = (8192.0 / wavelength - 1.0) / 3.0
    middle = (1.0 - blend) * base_freq / 8.0 + blend * base_freq
    return jnp.where(
        wavelength > 8192.0, base_freq / 8.0, jnp.where(wavelength < 2048.0, base_freq, middle)
    )


def moved(index, shift, sign=1):
    return (index % 4 + sign * shift[0] + 4) % 4 + 4 * ((index // 4) ^ shift[1])


def to_seq(block, shift, sign=1):
    return lax.ppermute(block, "seq", [(i, moved(i, shift, sign)) for i in range(SEQ)])


def to_samp(block, shift, other_core=0):
    pairs = [
        (2 * g + c, 2 * moved(g, shift) + (c ^ other_core)) for g in range(GROUPS) for c in range(2)
    ]
    return lax.ppermute(block, "samp", pairs)


def whole(memory_space=pltpu.VMEM):
    return pl.BlockSpec(memory_space=memory_space)


def project_kernel(places, *refs):
    rows, (w_own, w_other), outs = refs[:SEQ], refs[SEQ : SEQ + 2], refs[SEQ + 2 : -2]
    comp, weights = refs[-2:]
    depth = w_own.shape[0]
    weights[:depth, :] = w_own[...]
    weights[depth:, :] = w_other[...]
    gathered = jnp.concatenate([r[PROMPT_ROWS:, :] for r in rows], axis=0)
    n = gathered.shape[0]
    to_row = lax.broadcasted_iota(jnp.int32, (n, n), 0)
    from_row = lax.broadcasted_iota(jnp.int32, (n, n), 1)
    wanted = (to_row % GROUPS) * GROUPS + to_row // GROUPS
    order = jnp.where(from_row == wanted, 1.0, 0.0).astype(jnp.bfloat16)
    comp[...] = jnp.dot(order, gathered, preferred_element_type=jnp.float32)
    for k, out in enumerate(outs):
        g = places[k]
        parts = [r[pl.ds(pl.multiple_of(16 * g, 16), 16), :] for r in rows]
        parts.append(comp[pl.ds(pl.multiple_of(8 * g, 8), 8), :].astype(jnp.bfloat16))
        block = jnp.concatenate(parts, axis=0)
        product = jnp.dot(block, weights[...], preferred_element_type=jnp.float32)
        wide = block.astype(jnp.float32)
        squares = jnp.sum(wide * wide, axis=1, keepdims=True)
        high = squares.astype(jnp.bfloat16).astype(jnp.float32)
        lane = lax.broadcasted_iota(jnp.int32, (ROWS, HEAD), 1)
        extra = jnp.where(lane == 0, high, jnp.where(lane == 1, squares - high, 0.0))
        width = product.shape[1]
        out[:, :width] = product.astype(jnp.bfloat16)
        out[:, width:] = extra.astype(jnp.bfloat16)


def project(places, rows, w_own, w_other):
    width = w_own.shape[1]
    out = jax.ShapeDtypeStruct((ROWS, width + HEAD), jnp.bfloat16)
    return pl.pallas_call(
        project_kernel,
        out_shape=[out] * GROUPS,
        in_specs=[whole(pltpu.SMEM)] + [whole()] * (SEQ + 2),
        out_specs=[whole()] * GROUPS,
        scratch_shapes=[
            pltpu.VMEM((SEQ * GROUPS, 2 * w_own.shape[0]), jnp.float32),
            pltpu.VMEM((2 * w_own.shape[0], width), jnp.bfloat16),
        ],
        name="project",
    )(places, *rows, w_own, w_other)


def rotate_kernel(*refs):
    parts, cos_ref, sin_ref, q_ref, kv_ref = refs[:GROUPS], *refs[GROUPS:]
    width = (HEADS + 2) * HEAD
    tail = sum(p[:, width:].astype(jnp.float32) for p in parts)
    squares = tail[:, :1] + tail[:, 1:2]
    inv = lax.rsqrt(squares / FEATURES + NORM_EPS)
    cosine, sine = cos_ref[...], sin_ref[...]
    for h in range(HEADS + 2):
        columns = pl.ds(h * HEAD, HEAD)
        u = sum(p[:, columns].astype(jnp.float32) for p in parts) * inv
        if h <= HEADS:
            u = u * cosine + pltpu.roll(u, HEAD // 2, 1) * sine
        u = u.astype(jnp.bfloat16)
        if h < HEADS:
            q_ref[pl.ds(h * ROWS, ROWS), :] = u
        else:
            kv_ref[:, pl.ds((h - HEADS) * HEAD, HEAD)] = u


def rotate(parts, cosine, sine):
    return pl.pallas_call(
        rotate_kernel,
        out_shape=(
            jax.ShapeDtypeStruct((HEADS * ROWS, HEAD), jnp.bfloat16),
            jax.ShapeDtypeStruct((ROWS, 2 * HEAD), jnp.bfloat16),
        ),
        in_specs=[whole()] * (GROUPS + 2),
        out_specs=(whole(), whole()),
        name="rotate",
    )(*parts, cosine, sine)


def prefix_kernel(count, q_ref, kv_ref, acc_ref, max_ref, sum_ref, *, slots):
    step = pl.program_id(0)

    @pl.when(step == 0)
    def _():
        acc_ref[...] = jnp.zeros_like(acc_ref)
        max_ref[...] = jnp.full_like(max_ref, MASK_FILL)
        sum_ref[...] = jnp.zeros_like(sum_ref)

    first = step * slots

    def absorb(masked):
        keys, values = kv_ref[0, 0], kv_ref[1, 0]
        values = jnp.concatenate([values, jnp.ones_like(values)], axis=1)
        if masked:
            ids = first + lax.broadcasted_iota(jnp.int32, (1, slots), 1)
            bias = jnp.where(ids < count[0], 0.0, MASK_FILL)
        for h in range(HEADS):
            rows = pl.ds(h * ROWS, ROWS)
            scores = lax.dot_general(
                q_ref[rows, :], keys, LAST_DIMS, preferred_element_type=jnp.float32
            )
            if masked:
                scores = scores + bias
            old = max_ref[rows, :]
            new = jnp.maximum(old, jnp.max(scores, axis=1, keepdims=True))
            weights = jnp.exp2((scores - new[:, :1]) * LOG2_SCALE).astype(jnp.bfloat16)
            factor = jnp.exp2((old - new) * LOG2_SCALE)
            both = jnp.dot(weights, values, preferred_element_type=jnp.float32)
            acc_ref[rows, :] = acc_ref[rows, :] * factor + both[:, :HEAD]
            sum_ref[rows, :] = sum_ref[rows, :] * factor + both[:, HEAD:]
            max_ref[rows, :] = new

    @pl.when(first + slots <= count[0])
    def _():
        absorb(False)

    @pl.when((first < count[0]) & (first + slots > count[0]))
    def _():
        absorb(True)


def attend_prefix(count, queries, cache, slots=2048):
    n = queries.shape[0]
    state = jax.ShapeDtypeStruct((n, HEAD), jnp.float32)

    def cache_block(step, count):
        return (0, 0, jnp.minimum(step, lax.div(count[0] - 1, slots)), 0)

    return pl.pallas_call(
        functools.partial(prefix_kernel, slots=slots),
        out_shape=(state, state, state),
        grid_spec=pltpu.PrefetchScalarGridSpec(
            num_scalar_prefetch=1,
            grid=(cache.shape[2] // slots,),
            in_specs=[
                pl.BlockSpec((n, HEAD), lambda step, count: (0, 0)),
                pl.BlockSpec((2, 1, slots, HEAD), cache_block),
            ],
            out_specs=[pl.BlockSpec((n, HEAD), lambda step, count: (0, 0))] * 3,
        ),
        compiler_params=pltpu.CompilerParams(dimension_semantics=("arbitrary",)),
        name="prefix",
    )(count, queries, cache)


def finish_kernel(*refs):
    q_ref, acc_ref, max_ref, sum_ref, limit, low, high, ids, comp_ids = refs[:9]
    near, far, outs = refs[9:11], refs[11:25], refs[25:]
    blocks = [r[:PROMPT_ROWS, :] for r in near] + [r[...] for r in far]
    keys = jnp.concatenate([b[:, :HEAD] for b in blocks], axis=0)
    values = jnp.concatenate([b[:, HEAD:] for b in blocks], axis=0)
    values = jnp.concatenate([values, jnp.ones_like(values)], axis=1)
    comp = jnp.concatenate([r[PROMPT_ROWS:, :] for r in near], axis=0)
    comp_values = jnp.concatenate([comp[:, HEAD:], jnp.ones_like(comp[:, HEAD:])], axis=1)
    live = ids[...] <= limit[...]
    bias = jnp.where(live, 0.0, MASK_FILL)
    comp_live = (comp_ids[...] >= low[...]) & (comp_ids[...] <= high[...])
    comp_bias = jnp.where(comp_live, 0.0, MASK_FILL)
    for h in range(HEADS):
        rows = pl.ds(h * ROWS, ROWS)
        q = q_ref[rows, :]
        scores = lax.dot_general(q, keys, LAST_DIMS, preferred_element_type=jnp.float32) + bias
        comp_scores = (
            lax.dot_general(q, comp[:, :HEAD], LAST_DIMS, preferred_element_type=jnp.float32)
            + comp_bias
        )
        old = max_ref[rows, :]
        new = jnp.maximum(old, jnp.max(scores, axis=1, keepdims=True))
        new = jnp.maximum(new, jnp.max(comp_scores, axis=1, keepdims=True))
        weights = jnp.exp2((scores - new[:, :1]) * LOG2_SCALE).astype(jnp.bfloat16)
        comp_weights = jnp.exp2((comp_scores - new[:, :1]) * LOG2_SCALE).astype(jnp.bfloat16)
        factor = jnp.exp2((old - new) * LOG2_SCALE)
        both = jnp.dot(weights, values, preferred_element_type=jnp.float32)
        both = both + jnp.dot(comp_weights, comp_values, preferred_element_type=jnp.float32)
        context = acc_ref[rows, :] * factor + both[:, :HEAD]
        context = context / (sum_ref[rows, :] * factor + both[:, HEAD:])
        columns = pl.ds(h * HEAD, HEAD)
        for j, out in enumerate(outs):
            out[:16, columns] = context[16 * j : 16 * j + 16].astype(jnp.bfloat16)
            out[16:, columns] = context[PROMPT_ROWS:].astype(jnp.bfloat16)


def finish(queries, state, marks, near, far):
    out = jax.ShapeDtypeStruct((24, HEADS * HEAD), jnp.bfloat16)
    return pl.pallas_call(
        finish_kernel,
        out_shape=[out] * SEQ,
        in_specs=[whole()] * 25,
        out_specs=[whole()] * SEQ,
        name="finish",
    )(queries, *state, *marks, *near, *far)


def pack_kernel(*refs):
    blocks, out = refs[:SEQ], refs[SEQ]
    row = lax.broadcasted_iota(jnp.int32, (8, HEADS * HEAD), 0)
    comp = jnp.zeros((8, HEADS * HEAD), jnp.float32)
    for j, block in enumerate(blocks):
        out[pl.ds(16 * j, 16), :] = block[:16, :]
        comp = jnp.where(row == j, block[16:, :].astype(jnp.float32), comp)
    out[PROMPT_ROWS:, :] = comp.astype(jnp.bfloat16)


def pack(blocks):
    return pl.pallas_call(
        pack_kernel,
        out_shape=jax.ShapeDtypeStruct((ROWS, HEADS * HEAD), jnp.bfloat16),
        in_specs=[whole()] * SEQ,
        out_specs=whole(),
        name="pack",
    )(*blocks)


def output_kernel(place, order, prompt_rest, comp_rest, *refs):
    n = 2 * GROUPS
    blocks, weights, (prompt_out, comp_out) = refs[:n], refs[n : n + SEQ], refs[n + SEQ : n + SEQ + 2]
    held, matrix, block_sem, matrix_sem = refs[n + SEQ + 2 :]
    copies = [
        pltpu.make_async_copy(b, held.at[i], block_sem.at[i]) for i, b in enumerate(blocks)
    ]
    loads = [
        pltpu.make_async_copy(w, matrix.at[j], matrix_sem.at[j]) for j, w in enumerate(weights)
    ]
    for copy in copies + loads:
        copy.start()
    for copy in copies:
        copy.wait()
    comp = jnp.concatenate([held[i, PROMPT_ROWS:, :] for i in range(n)], axis=0)
    comp = jnp.dot(order[...], comp, preferred_element_type=jnp.float32).astype(jnp.bfloat16)
    total = jnp.zeros((16 * n + n, prompt_out.shape[1]), jnp.float32)
    for j in range(SEQ):
        left = [held[i, pl.ds(16 * j, 16), :] for i in range(n)]
        left = jnp.concatenate(left + [comp[n * j : n * j + n]], axis=0)
        loads[j].wait()
        total = total + jnp.dot(left, matrix[j], preferred_element_type=jnp.float32)
    for i in range(n):
        at = pl.ds(pl.multiple_of(16 * place[i], 16), 16)
        rest = prompt_rest[at, :].astype(jnp.float32)
        prompt_out[at, :] = (total[16 * i : 16 * i + 16] + rest).astype(jnp.bfloat16)
    rest = comp_rest[...].astype(jnp.float32)
    comp_out[...] = (total[16 * n :] + rest).astype(jnp.bfloat16)


def output(place, order, prompt_rest, comp_rest, blocks, weights):
    n = len(blocks)
    width = prompt_rest.shape[1]
    return pl.pallas_call(
        output_kernel,
        out_shape=(
            jax.ShapeDtypeStruct((16 * n, width), jnp.bfloat16),
            jax.ShapeDtypeStruct((n, width), jnp.bfloat16),
        ),
        in_specs=[whole(pltpu.SMEM), whole(), whole(), whole()]
        + [whole(pl.ANY)] * (n + SEQ),
        out_specs=(whole(), whole()),
        scratch_shapes=[
            pltpu.VMEM((n, ROWS, HEADS * HEAD), jnp.bfloat16),
            pltpu.VMEM((SEQ, HEADS * HEAD, width), jnp.bfloat16),
            pltpu.SemaphoreType.DMA((n,)),
            pltpu.SemaphoreType.DMA((SEQ,)),
        ],
        name="output",
    )(place, order, prompt_rest, comp_rest, *blocks, *weights)


def body(
    prompt_ids,
    comp_ids,
    prefix_len,
    prompt_offset,
    embed_table,
    attn_gain,
    query_key_value_weight,
    w_out,
    key_value_cache,
):
    seq_index = lax.axis_index("seq")
    samp_index = lax.axis_index("samp")
    group, core = samp_index // 2, samp_index % 2
    vocab_rows, width = embed_table.shape

    scaled = query_key_value_weight.astype(jnp.float32) * attn_gain.astype(jnp.float32)[:, None]
    scaled = scaled.astype(jnp.bfloat16)
    scaled_other = to_samp(scaled, (0, 0), 1)
    out_flip = to_seq(w_out, (0, 1))

    by_prompt = prompt_ids.reshape(SEQ, GROUPS, 2, 16).transpose(0, 2, 1, 3).reshape(SEQ, 2, 128)
    by_comp = comp_ids.reshape(SEQ, GROUPS, 2).transpose(0, 2, 1)
    row_ids = jnp.concatenate([by_prompt, by_comp], axis=2).reshape(SEQ, 2 * ROWS)
    row_ids = row_ids - seq_index * vocab_rows
    arrived = []
    for shift in SHIFTS[1:] + SHIFTS[:1]:
        local = lax.dynamic_index_in_dim(row_ids, moved(seq_index, shift), 0, keepdims=False)
        inside = (local >= 0) & (local < vocab_rows)
        picked = jnp.take(embed_table, jnp.clip(local, 0, vocab_rows - 1), axis=0)
        part = jnp.where(inside[:, None], picked, jnp.zeros((), jnp.bfloat16))
        arrived.append(to_seq(part, shift) if shift != (0, 0) else part)
    embedded = sum(a.astype(jnp.float32) for a in arrived).astype(jnp.bfloat16)

    kept = lax.dynamic_slice_in_dim(embedded, core * ROWS, ROWS, 0)
    given = lax.dynamic_slice_in_dim(embedded, (1 - core) * ROWS, ROWS, 0)
    mine = jnp.concatenate([kept, to_samp(given, (0, 0), 1)], axis=1)
    rows = [mine] + [to_seq(mine, shift) for shift in SHIFTS[1:]]

    places = jnp.stack([moved(group, shift) for shift in SHIFTS]).astype(jnp.int32)
    partial = project(places, rows, scaled, scaled_other)
    parts = [partial[0]] + [to_samp(b, shift) for b, shift in zip(partial[1:], SHIFTS[1:])]

    source = jnp.stack([moved(seq_index, shift, -1) for shift in SHIFTS]).astype(jnp.int32)
    within = jnp.arange(16, dtype=jnp.int32)

    def prompt_rows(samp):
        return (256 * source[:, None] + 16 * samp + within[None, :]).reshape(PROMPT_ROWS)

    def comp_marks(samp):
        return COMP_ID + 2 * source + samp % 2

    start = prompt_offset[0]
    own_prompt = prompt_rows(samp_index)
    comp_pos = jnp.broadcast_to(start + 2048 + core, (SEQ,))
    position = jnp.concatenate([start + own_prompt, comp_pos]).astype(jnp.float32)
    angles = position[:, None] * rope_freqs(HEAD)[None, :]
    cosine, sine = jnp.cos(angles), jnp.sin(angles)
    cosine = jnp.concatenate([cosine, cosine], axis=1)
    sine = jnp.concatenate([-sine, sine], axis=1)
    queries, own_kv = rotate(parts, cosine, sine)

    near = [own_kv, to_samp(own_kv, (0, 0), 1)]
    far, from_samp = [], []
    for shift in SHIFTS[1:]:
        for other in (0, 1):
            far.append(to_samp(own_kv[:PROMPT_ROWS], shift, other))
            from_samp.append(2 * moved(group, shift, -1) + (core ^ other))
    state = attend_prefix(prefix_len, queries, key_value_cache)

    other_samp = 2 * group + (1 - core)
    ids = jnp.concatenate([prompt_rows(m) for m in [samp_index, other_samp] + from_samp])
    comp_key_ids = jnp.concatenate([comp_marks(samp_index), comp_marks(other_samp)])
    none = jnp.full((PROMPT_ROWS,), -1, jnp.int32)
    limit = jnp.concatenate([own_prompt, jnp.full((SEQ,), 2048, jnp.int32)])
    low = jnp.concatenate([none, COMP_ID + 2 * source])
    high = jnp.concatenate([none, comp_marks(samp_index)])
    marks = (limit[:, None], low[:, None], high[:, None], ids[None, :], comp_key_ids[None, :])
    context = finish(queries, state, marks, near, far)

    w_own, w_flip, _ = lax.optimization_barrier((w_out, out_flip, rows[-1]))
    w_next, w_next_flip = to_seq(w_own, (3, 0)), to_seq(w_flip, (3, 0))
    w_last, w_last_flip = to_seq(w_own, (1, 0)), to_seq(w_flip, (1, 0))
    weights = {
        (0, 0): w_own,
        (0, 1): w_flip,
        (1, 0): w_next,
        (1, 1): w_next_flip,
        (3, 0): w_last,
        (3, 1): w_last_flip,
        (2, 0): to_seq(w_next, (3, 0)),
        (2, 1): to_seq(w_last_flip, (1, 0)),
    }

    headed = [context[0]]
    headed += [to_seq(b, shift, -1) for b, shift in zip(context[1:], SHIFTS[1:])]
    packed = pack(headed)
    same = [packed] + [to_samp(packed, shift) for shift in SHIFTS[1:]]
    crossed = [to_samp(b, (0, 0), 1) for b in same]
    came = jnp.stack([moved(group, shift, -1) for shift in SHIFTS]).astype(jnp.int32)
    place = jnp.concatenate([2 * came + core, 2 * came + (1 - core)])
    to_row = jnp.arange(128, dtype=jnp.int32)
    to_shift, to_samp_row = to_row // 16, to_row % 16
    from_place = place[to_row // 8]
    order = (to_shift[:, None] == (to_row % 8)[None, :]) & (
        to_samp_row[:, None] == from_place[None, :]
    )
    halves = embedded.reshape(2, ROWS, width)
    prompt_rest = halves[:, :PROMPT_ROWS].reshape(2, GROUPS, 16, width)
    prompt_rest = prompt_rest.transpose(1, 0, 2, 3).reshape(256, width)
    comp_rest = halves[:, PROMPT_ROWS:].transpose(1, 0, 2).reshape(16, width)
    prompt_out, comp_out = output(
        place,
        order.astype(jnp.bfloat16),
        prompt_rest,
        comp_rest,
        same + crossed,
        [weights[shift] for shift in SHIFTS],
    )
    return prompt_out, comp_out.reshape(8, 2, width)


def solution(mesh):
    placed = (
        P(),
        P(),
        P(),
        P(),
        P("seq", "samp"),
        P("samp"),
        P("samp", "seq"),
        P("seq", "samp"),
        P(None, "seq", None, None),
    )
    return jax.shard_map(
        body,
        mesh=mesh,
        in_specs=placed,
        out_specs=(P("seq", "samp"), P("seq", None, "samp")),
        check_vma=False,
    )
```

```python
import functools
import math

import jax
import jax.numpy as jnp
from jax import lax
from jax.experimental import pallas as pl
from jax.experimental.pallas import tpu as pltpu
from jax.sharding import PartitionSpec as P


NORM_EPS = 1e-05
MASK_FILL = -1e30
HEAD = 128
HEADS = 8
SEQ = 8
GROUPS = 8
SAMP = 16
ROWS = 136
PROMPT_ROWS = 128
FEATURES = 8192
LOG2_SCALE = math.log2(math.e) / math.sqrt(HEAD)
LAST_DIMS = (((1,), (1,)), ((), ()))

SAME_CORE = [[2 * g + c for g in range(GROUPS)] for c in range(2)]
SEQ_CORE = [[SAMP * s + 2 * g + c for s in range(SEQ) for c in range(2)] for g in range(GROUPS)]
SEQ_GROUP = [[SAMP * s + 2 * g + c for s in range(SEQ) for g in range(GROUPS)] for c in range(2)]
SHIFTS = ((0, 0), (0, 1), (1, 0), (1, 1), (3, 0), (3, 1), (2, 0), (2, 1))


def rope_freqs(head_dim):
    half_dim = head_dim // 2
    dim_index = jnp.arange(half_dim, dtype=jnp.float32)
    base_freq = 1.0 / jnp.power(500000.0, 2.0 * dim_index / head_dim)
    wavelength = 2.0 * math.pi / base_freq
    blend = (8192.0 / wavelength - 1.0) / 3.0
    middle = (1.0 - blend) * base_freq / 8.0 + blend * base_freq
    return jnp.where(
        wavelength > 8192.0, base_freq / 8.0, jnp.where(wavelength < 2048.0, base_freq, middle)
    )


def moved(index, shift, sign=1):
    return (index % 4 + sign * shift[0] + 4) % 4 + 4 * ((index // 4) ^ shift[1])


def to_seq(block, shift):
    return lax.ppermute(block, "seq", [(i, moved(i, shift)) for i in range(SEQ)])


def to_other_core(block):
    return lax.ppermute(block, "samp", [(i, i ^ 1) for i in range(SAMP)])


def exchange(blocks, axes, groups=None):
    return lax.all_to_all(blocks, axes, 0, 0, tiled=True, axis_index_groups=groups)


def whole(memory_space=pltpu.VMEM):
    return pl.BlockSpec(memory_space=memory_space)


def merge_kernel(place, got, owner, copies, kept, given):
    core = place[1]
    halves = []
    for c in range(2):
        total = jnp.zeros(kept.shape, jnp.float32)
        for s in range(SEQ):
            total = jnp.where(owner[...] == s, got[2 * s + c].astype(jnp.float32), total)
        halves.append(total.astype(jnp.bfloat16))
    mine = jnp.concatenate(halves, axis=1)
    for s in range(SEQ):
        copies[s] = mine

    @pl.when(core == 0)
    def _():
        kept[...] = halves[0]
        given[...] = halves[1]

    @pl.when(core == 1)
    def _():
        kept[...] = halves[1]
        given[...] = halves[0]


def merge(place, got, owner):
    width = got.shape[2]
    half = jax.ShapeDtypeStruct((ROWS, width), jnp.bfloat16)
    return pl.pallas_call(
        merge_kernel,
        out_shape=(jax.ShapeDtypeStruct((SEQ, ROWS, 2 * width), jnp.bfloat16), half, half),
        in_specs=[whole(pltpu.SMEM), whole(), whole()],
        out_specs=(whole(), whole(), whole()),
        name="merge",
    )(place, got, owner)


def project_kernel(place, rows, w_own, w_other, out, comp, weights):
    core = place[1]
    depth, width = w_own.shape
    weights[pl.ds(pl.multiple_of(core * depth, depth), depth), :] = w_own[...]
    weights[pl.ds(pl.multiple_of((1 - core) * depth, depth), depth), :] = w_other[...]
    gathered = jnp.concatenate([rows[s, PROMPT_ROWS:, :] for s in range(SEQ)], axis=0)
    n = SEQ * GROUPS
    to_row = lax.broadcasted_iota(jnp.int32, (n, n), 0)
    from_row = lax.broadcasted_iota(jnp.int32, (n, n), 1)
    wanted = (to_row % SEQ) * GROUPS + to_row // SEQ
    order = jnp.where(from_row == wanted, 1.0, 0.0).astype(jnp.bfloat16)
    comp[...] = jnp.dot(order, gathered, preferred_element_type=jnp.float32)

    def block_of(g, carry):
        parts = [rows[s, pl.ds(pl.multiple_of(16 * g, 16), 16), :] for s in range(SEQ)]
        parts.append(comp[pl.ds(pl.multiple_of(8 * g, 8), 8), :].astype(jnp.bfloat16))
        block = jnp.concatenate(parts, axis=0)
        product = jnp.dot(block, weights[...], preferred_element_type=jnp.float32)
        wide = block.astype(jnp.float32)
        squares = jnp.sum(wide * wide, axis=1, keepdims=True)
        high = squares.astype(jnp.bfloat16).astype(jnp.float32)
        lane = lax.broadcasted_iota(jnp.int32, (ROWS, HEAD), 1)
        extra = jnp.where(lane == 0, high, jnp.where(lane == 1, squares - high, 0.0))
        out[g, :, :width] = product.astype(jnp.bfloat16)
        out[g, :, width:] = extra.astype(jnp.bfloat16)
        return carry

    lax.fori_loop(0, GROUPS, block_of, 0)


def project(place, rows, w_own, w_other):
    depth, width = w_own.shape
    return pl.pallas_call(
        project_kernel,
        out_shape=jax.ShapeDtypeStruct((GROUPS, ROWS, width + HEAD), jnp.bfloat16),
        in_specs=[whole(pltpu.SMEM), whole(), whole(), whole()],
        out_specs=whole(),
        scratch_shapes=[
            pltpu.VMEM((SEQ * GROUPS, 2 * depth), jnp.float32),
            pltpu.VMEM((2 * depth, width), jnp.bfloat16),
        ],
        name="project",
    )(place, rows, w_own, w_other)


def rotate_kernel(parts, cos_ref, sin_ref, q_ref, kv_ref):
    width = (HEADS + 2) * HEAD
    tail = sum(parts[g, :, width:].astype(jnp.float32) for g in range(GROUPS))
    squares = tail[:, :1] + tail[:, 1:2]
    inv = lax.rsqrt(squares / FEATURES + NORM_EPS)
    cosine, sine = cos_ref[...], sin_ref[...]
    for h in range(HEADS + 2):
        columns = pl.ds(h * HEAD, HEAD)
        u = sum(parts[g, :, columns].astype(jnp.float32) for g in range(GROUPS)) * inv
        if h <= HEADS:
            u = u * cosine + pltpu.roll(u, HEAD // 2, 1) * sine
        u = u.astype(jnp.bfloat16)
        if h < HEADS:
            q_ref[pl.ds(h * ROWS, ROWS), :] = u
        else:
            for m in range(SAMP):
                kv_ref[m, :, pl.ds((h - HEADS) * HEAD, HEAD)] = u


def rotate(parts, cosine, sine):
    return pl.pallas_call(
        rotate_kernel,
        out_shape=(
            jax.ShapeDtypeStruct((HEADS * ROWS, HEAD), jnp.bfloat16),
            jax.ShapeDtypeStruct((SAMP, ROWS, 2 * HEAD), jnp.bfloat16),
        ),
        in_specs=[whole()] * 3,
        out_specs=(whole(), whole()),
        name="rotate",
    )(parts, cosine, sine)


def prefix_kernel(count, q_ref, kv_ref, acc_ref, max_ref, sum_ref, *, slots):
    step = pl.program_id(0)

    @pl.when(step == 0)
    def _():
        acc_ref[...] = jnp.zeros_like(acc_ref)
        max_ref[...] = jnp.full_like(max_ref, MASK_FILL)
        sum_ref[...] = jnp.zeros_like(sum_ref)

    first = step * slots

    def absorb(masked):
        keys, values = kv_ref[0, 0], kv_ref[1, 0]
        values = jnp.concatenate([values, jnp.ones_like(values)], axis=1)
        if masked:
            ids = first + lax.broadcasted_iota(jnp.int32, (1, slots), 1)
            bias = jnp.where(ids < count[0], 0.0, MASK_FILL)
        for h in range(HEADS):
            rows = pl.ds(h * ROWS, ROWS)
            scores = lax.dot_general(
                q_ref[rows, :], keys, LAST_DIMS, preferred_element_type=jnp.float32
            )
            if masked:
                scores = scores + bias
            old = max_ref[rows, :]
            new = jnp.maximum(old, jnp.max(scores, axis=1, keepdims=True))
            weights = jnp.exp2((scores - new[:, :1]) * LOG2_SCALE).astype(jnp.bfloat16)
            factor = jnp.exp2((old - new) * LOG2_SCALE)
            both = jnp.dot(weights, values, preferred_element_type=jnp.float32)
            acc_ref[rows, :] = acc_ref[rows, :] * factor + both[:, :HEAD]
            sum_ref[rows, :] = sum_ref[rows, :] * factor + both[:, HEAD:]
            max_ref[rows, :] = new

    @pl.when(first + slots <= count[0])
    def _():
        absorb(False)

    @pl.when((first < count[0]) & (first + slots > count[0]))
    def _():
        absorb(True)


def attend_prefix(count, queries, cache, slots=2048):
    n = queries.shape[0]
    state = jax.ShapeDtypeStruct((n, HEAD), jnp.float32)

    def cache_block(step, count):
        return (0, 0, jnp.minimum(step, lax.div(count[0] - 1, slots)), 0)

    return pl.pallas_call(
        functools.partial(prefix_kernel, slots=slots),
        out_shape=(state, state, state),
        grid_spec=pltpu.PrefetchScalarGridSpec(
            num_scalar_prefetch=1,
            grid=(cache.shape[2] // slots,),
            in_specs=[
                pl.BlockSpec((n, HEAD), lambda step, count: (0, 0)),
                pl.BlockSpec((2, 1, slots, HEAD), cache_block),
            ],
            out_specs=[pl.BlockSpec((n, HEAD), lambda step, count: (0, 0))] * 3,
        ),
        compiler_params=pltpu.CompilerParams(dimension_semantics=("arbitrary",)),
        name="prefix",
    )(count, queries, cache)


def finish_kernel(place, q_ref, acc_ref, max_ref, sum_ref, kv, out, block, comp_block):
    group, core = place[0], place[1]
    keys = jnp.concatenate([kv[m, :PROMPT_ROWS, :HEAD] for m in range(SAMP)], axis=0)
    values = jnp.concatenate([kv[m, :PROMPT_ROWS, HEAD:] for m in range(SAMP)], axis=0)
    values = jnp.concatenate([values, jnp.ones_like(values)], axis=1)
    first = 2 * (group - group % 2) + core
    comp = jnp.concatenate([kv[first, PROMPT_ROWS:, :], kv[first + 2, PROMPT_ROWS:, :]], axis=0)
    comp_values = jnp.concatenate([comp[:, HEAD:], jnp.ones_like(comp[:, HEAD:])], axis=1)
    n = keys.shape[0]
    column = lax.broadcasted_iota(jnp.int32, (1, n), 1)
    samp = column // PROMPT_ROWS
    key_id = 256 * (column // 16 % SEQ) + 128 * (samp % 2) + 16 * (samp // 2) + column % 16
    row = lax.broadcasted_iota(jnp.int32, (ROWS, 1), 0)
    own_id = 256 * (row // 16) + 128 * core + 16 * group + row % 16
    limit = jnp.where(row < PROMPT_ROWS, own_id, n)
    bias = jnp.where(key_id <= limit, 0.0, MASK_FILL)
    column = lax.broadcasted_iota(jnp.int32, (1, 2 * SEQ), 1)
    live = (column % SEQ == row - PROMPT_ROWS) & (column // SEQ <= group % 2)
    comp_bias = jnp.where(live, 0.0, MASK_FILL)
    for h in range(HEADS):
        rows = pl.ds(h * ROWS, ROWS)
        q = q_ref[rows, :]
        scores = lax.dot_general(q, keys, LAST_DIMS, preferred_element_type=jnp.float32) + bias
        comp_scores = (
            lax.dot_general(q, comp[:, :HEAD], LAST_DIMS, preferred_element_type=jnp.float32)
            + comp_bias
        )
        old = max_ref[rows, :]
        new = jnp.maximum(old, jnp.max(scores, axis=1, keepdims=True))
        new = jnp.maximum(new, jnp.max(comp_scores, axis=1, keepdims=True))
        weights = jnp.exp2((scores - new[:, :1]) * LOG2_SCALE).astype(jnp.bfloat16)
        comp_weights = jnp.exp2((comp_scores - new[:, :1]) * LOG2_SCALE).astype(jnp.bfloat16)
        factor = jnp.exp2((old - new) * LOG2_SCALE)
        both = jnp.dot(weights, values, preferred_element_type=jnp.float32)
        both = both + jnp.dot(comp_weights, comp_values, preferred_element_type=jnp.float32)
        context = acc_ref[rows, :] * factor + both[:, :HEAD]
        context = context / (sum_ref[rows, :] * factor + both[:, HEAD:])
        for s in range(SEQ):
            block[s, pl.ds(16 * h, 16), :] = context[16 * s : 16 * s + 16].astype(jnp.bfloat16)
            comp_block[s, pl.ds(h, 1), :] = context[PROMPT_ROWS + s : PROMPT_ROWS + s + 1]
    for s in range(SEQ):
        block[s, PROMPT_ROWS:, :] = comp_block[s].astype(jnp.bfloat16)

    def copy_of(g, carry):
        for s in range(SEQ):
            out[s * GROUPS + g] = block[s]
        return carry

    lax.fori_loop(0, GROUPS, copy_of, 0)


def finish(place, queries, state, kv):
    return pl.pallas_call(
        finish_kernel,
        out_shape=jax.ShapeDtypeStruct((SEQ * GROUPS, ROWS, HEAD), jnp.bfloat16),
        in_specs=[whole(pltpu.SMEM)] + [whole()] * 5,
        out_specs=whole(),
        scratch_shapes=[
            pltpu.VMEM((SEQ, ROWS, HEAD), jnp.bfloat16),
            pltpu.VMEM((SEQ, HEADS, HEAD), jnp.float32),
        ],
        name="finish",
    )(place, queries, *state, kv)


def output_kernel(place, source, kept, came, same, crossed, *refs):
    weights, (prompt_out, comp_out) = refs[:SEQ], refs[SEQ:]
    core = place[1]
    blocks = (same, crossed)
    n = SAMP * HEADS
    to_row = lax.broadcasted_iota(jnp.int32, (n, n), 0)
    from_row = lax.broadcasted_iota(jnp.int32, (n, n), 1)
    head, out_row = to_row // SAMP, to_row % SAMP
    crossing = (out_row // GROUPS + core) % 2
    wanted = crossing * (GROUPS * HEADS) + (out_row % GROUPS) * HEADS + head
    order = jnp.where(from_row == wanted, 1.0, 0.0).astype(jnp.bfloat16)
    total = jnp.zeros((SAMP * 17, prompt_out.shape[1]), jnp.float32)
    for j in range(SEQ):
        first = source[j] * GROUPS
        left = []
        for b in blocks:
            for g in range(GROUPS):
                parts = [b[first + g, pl.ds(16 * h, 16), :] for h in range(HEADS)]
                left.append(jnp.concatenate(parts, axis=1))
        comp = [b[first + g, PROMPT_ROWS:, :] for b in blocks for g in range(GROUPS)]
        comp = jnp.concatenate(comp, axis=0)
        comp = jnp.dot(order, comp, preferred_element_type=jnp.float32).astype(jnp.bfloat16)
        parts = [comp[SAMP * h : SAMP * h + SAMP] for h in range(HEADS)]
        left.append(jnp.concatenate(parts, axis=1))
        left = jnp.concatenate(left, axis=0)
        total = total + jnp.dot(left, weights[j][...], preferred_element_type=jnp.float32)
    rests = (kept, came)
    for r in range(2):
        at = pl.ds(pl.multiple_of(((core + r) % 2) * PROMPT_ROWS, PROMPT_ROWS), PROMPT_ROWS)
        rest = rests[r][:PROMPT_ROWS, :].astype(jnp.float32)
        prompt_out[at, :] = (total[PROMPT_ROWS * r : PROMPT_ROWS * (r + 1)] + rest).astype(
            jnp.bfloat16
        )
    low = jnp.concatenate([kept[PROMPT_ROWS:, :], came[PROMPT_ROWS:, :]], axis=0)
    high = jnp.concatenate([came[PROMPT_ROWS:, :], kept[PROMPT_ROWS:, :]], axis=0)
    rest = jnp.where(core == 0, low.astype(jnp.float32), high.astype(jnp.float32))
    comp_out[...] = (total[2 * PROMPT_ROWS :] + rest).astype(jnp.bfloat16)


def output(place, source, kept, came, same, crossed, weights):
    width = kept.shape[1]
    return pl.pallas_call(
        output_kernel,
        out_shape=(
            jax.ShapeDtypeStruct((2 * PROMPT_ROWS, width), jnp.bfloat16),
            jax.ShapeDtypeStruct((SAMP, width), jnp.bfloat16),
        ),
        in_specs=[whole(pltpu.SMEM)] * 2 + [whole()] * (4 + SEQ),
        out_specs=(whole(), whole()),
        name="output",
    )(place, source, kept, came, same, crossed, *weights)


def body(
    prompt_ids,
    comp_ids,
    prefix_len,
    prompt_offset,
    embed_table,
    attn_gain,
    query_key_value_weight,
    w_out,
    key_value_cache,
):
    seq_index = lax.axis_index("seq")
    samp_index = lax.axis_index("samp")
    group, core = samp_index // 2, samp_index % 2
    place = jnp.stack([group, core]).astype(jnp.int32)
    vocab_rows, width = embed_table.shape

    ids = [prompt_ids.reshape(SEQ, 2, PROMPT_ROWS), comp_ids.reshape(SEQ, 2, GROUPS)]
    ids = jnp.concatenate(ids, axis=2)
    local = jnp.clip(ids.reshape(-1) - seq_index * vocab_rows, 0, vocab_rows - 1)
    picked = jnp.take(embed_table, local, axis=0).reshape(2 * SEQ, ROWS, width)
    got = exchange(picked, ("seq", "samp"), SEQ_CORE)
    own_ids = lax.dynamic_index_in_dim(ids.reshape(-1, ROWS), 2 * seq_index + core, 0, keepdims=False)
    copies, kept, given = merge(place, got, (own_ids // vocab_rows)[:, None])

    scaled = query_key_value_weight.astype(jnp.float32) * attn_gain.astype(jnp.float32)[:, None]
    scaled = scaled.astype(jnp.bfloat16)
    scaled_other = to_other_core(scaled)
    out_flip = to_seq(w_out, (0, 1))

    rows = exchange(copies, "seq")
    came = to_other_core(given)
    partial = project(place, rows, scaled, scaled_other)
    parts = exchange(partial, "samp", SAME_CORE)

    w_own, w_flip, _ = lax.optimization_barrier((w_out, out_flip, rows))
    w_next, w_next_flip = to_seq(w_own, (3, 0)), to_seq(w_flip, (3, 0))
    w_last, w_last_flip = to_seq(w_own, (1, 0)), to_seq(w_flip, (1, 0))
    w_far, w_far_flip = to_seq(w_next, (3, 0)), to_seq(w_last_flip, (1, 0))
    weights = [w_own, w_flip, w_next, w_next_flip, w_last, w_last_flip, w_far, w_far_flip]

    row = jnp.arange(ROWS, dtype=jnp.int32)
    own_prompt = 256 * (row // 16) + 128 * core + 16 * group + row % 16
    position = jnp.where(row < PROMPT_ROWS, own_prompt, 2048 + group % 2) + prompt_offset[0]
    angles = position.astype(jnp.float32)[:, None] * rope_freqs(HEAD)[None, :]
    cosine, sine = jnp.cos(angles), jnp.sin(angles)
    cosine = jnp.concatenate([cosine, cosine], axis=1)
    sine = jnp.concatenate([-sine, sine], axis=1)
    queries, kv = rotate(parts, cosine, sine)
    all_kv = exchange(kv, "samp")
    state = attend_prefix(prefix_len, queries, key_value_cache)
    context = finish(place, queries, state, all_kv)

    same = exchange(context, ("seq", "samp"), SEQ_GROUP)
    crossed = to_other_core(same)
    source = jnp.stack([moved(seq_index, shift) for shift in SHIFTS]).astype(jnp.int32)
    prompt_out, comp_out = output(place, source, kept, came, same, crossed, weights)
    return prompt_out, comp_out.reshape(8, 2, width)


def solution(mesh):
    placed = (
        P(),
        P(),
        P(),
        P(),
        P("seq", "samp"),
        P("samp"),
        P("samp", "seq"),
        P("seq", "samp"),
        P(None, "seq", None, None),
    )
    return jax.shard_map(
        body,
        mesh=mesh,
        in_specs=placed,
        out_specs=(P("seq", "samp"), P("seq", None, "samp")),
        check_vma=False,
    )
```

```python
import functools
import math

import jax
import jax.numpy as jnp
from jax import lax
from jax.experimental import pallas as pl
from jax.experimental.pallas import tpu as pltpu
from jax.sharding import PartitionSpec as P


NORM_EPS = 1e-05
MASK_FILL = -1e30
HEAD = 128
HEADS = 8
SEQ = 8
GROUPS = 8
SAMP = 16
ROWS = 136
PROMPT_ROWS = 128
FEATURES = 8192
LOG2_SCALE = math.log2(math.e) / math.sqrt(HEAD)
LAST_DIMS = (((1,), (1,)), ((), ()))

SAME_CORE = [[2 * g + c for g in range(GROUPS)] for c in range(2)]
SEQ_CORE = [[SAMP * s + 2 * g + c for s in range(SEQ) for c in range(2)] for g in range(GROUPS)]
SEQ_GROUP = [[SAMP * s + 2 * g + c for s in range(SEQ) for g in range(GROUPS)] for c in range(2)]
SHIFTS = ((0, 0), (0, 1), (1, 0), (1, 1), (3, 0), (3, 1), (2, 0), (2, 1))


def rope_freqs(head_dim):
    half_dim = head_dim // 2
    dim_index = jnp.arange(half_dim, dtype=jnp.float32)
    base_freq = 1.0 / jnp.power(500000.0, 2.0 * dim_index / head_dim)
    wavelength = 2.0 * math.pi / base_freq
    blend = (8192.0 / wavelength - 1.0) / 3.0
    middle = (1.0 - blend) * base_freq / 8.0 + blend * base_freq
    return jnp.where(
        wavelength > 8192.0, base_freq / 8.0, jnp.where(wavelength < 2048.0, base_freq, middle)
    )


def moved(index, shift, sign=1):
    return (index % 4 + sign * shift[0] + 4) % 4 + 4 * ((index // 4) ^ shift[1])


def to_seq(block, shift):
    return lax.ppermute(block, "seq", [(i, moved(i, shift)) for i in range(SEQ)])


def to_other_core(block):
    return lax.ppermute(block, "samp", [(i, i ^ 1) for i in range(SAMP)])


def exchange(blocks, axes, groups=None):
    return lax.all_to_all(blocks, axes, 0, 0, tiled=True, axis_index_groups=groups)


def whole(memory_space=pltpu.VMEM):
    return pl.BlockSpec(memory_space=memory_space)


def merge_kernel(place, got, owner, copies, kept, given, held, sem):
    core = place[1]
    halves = []
    for c in range(2):
        total = jnp.zeros(kept.shape, jnp.float32)
        for s in range(SEQ):
            total = jnp.where(owner[...] == s, got[2 * s + c].astype(jnp.float32), total)
        halves.append(total.astype(jnp.bfloat16))
    held[...] = jnp.concatenate(halves, axis=1)
    sends = [pltpu.make_async_copy(held, copies.at[s], sem.at[s]) for s in range(SEQ)]
    for send in sends:
        send.start()

    @pl.when(core == 0)
    def _():
        kept[...] = halves[0]
        given[...] = halves[1]

    @pl.when(core == 1)
    def _():
        kept[...] = halves[1]
        given[...] = halves[0]

    for send in sends:
        send.wait()


def merge(place, got, owner):
    width = got.shape[2]
    half = jax.ShapeDtypeStruct((ROWS, width), jnp.bfloat16)
    return pl.pallas_call(
        merge_kernel,
        out_shape=(pltpu.HBM((SEQ, ROWS, 2 * width), jnp.bfloat16), half, half),
        in_specs=[whole(pltpu.SMEM), whole(), whole()],
        out_specs=(whole(pltpu.HBM), whole(), whole()),
        scratch_shapes=[
            pltpu.VMEM((ROWS, 2 * width), jnp.bfloat16),
            pltpu.SemaphoreType.DMA((SEQ,)),
        ],
        compiler_params=pltpu.CompilerParams(vmem_limit_bytes=16 << 20),
        name="merge",
    )(place, got, owner)


def project_kernel(place, rows, w_own, w_other, out, comp, weights, held, sem):
    core = place[1]
    depth, width = w_own.shape
    weights[pl.ds(pl.multiple_of(core * depth, depth), depth), :] = w_own[...]
    weights[pl.ds(pl.multiple_of((1 - core) * depth, depth), depth), :] = w_other[...]
    gathered = jnp.concatenate([rows[s, PROMPT_ROWS:, :] for s in range(SEQ)], axis=0)
    n = SEQ * GROUPS
    to_row = lax.broadcasted_iota(jnp.int32, (n, n), 0)
    from_row = lax.broadcasted_iota(jnp.int32, (n, n), 1)
    wanted = (to_row % SEQ) * GROUPS + to_row // SEQ
    order = jnp.where(from_row == wanted, 1.0, 0.0).astype(jnp.bfloat16)
    comp[...] = jnp.dot(order, gathered, preferred_element_type=jnp.float32)

    def send(g):
        return pltpu.make_async_copy(held.at[g], out.at[g], sem.at[g])

    def block_of(g, carry):
        parts = [rows[s, pl.ds(pl.multiple_of(16 * g, 16), 16), :] for s in range(SEQ)]
        parts.append(comp[pl.ds(pl.multiple_of(8 * g, 8), 8), :].astype(jnp.bfloat16))
        block = jnp.concatenate(parts, axis=0)
        product = jnp.dot(block, weights[...], preferred_element_type=jnp.float32)
        wide = block.astype(jnp.float32)
        squares = jnp.sum(wide * wide, axis=1, keepdims=True)
        high = squares.astype(jnp.bfloat16).astype(jnp.float32)
        lane = lax.broadcasted_iota(jnp.int32, (ROWS, HEAD), 1)
        extra = jnp.where(lane == 0, high, jnp.where(lane == 1, squares - high, 0.0))
        held[g, :, :width] = product.astype(jnp.bfloat16)
        held[g, :, width:] = extra.astype(jnp.bfloat16)
        send(g).start()
        return carry

    lax.fori_loop(0, GROUPS, block_of, 0)
    for g in range(GROUPS):
        send(g).wait()


def project(place, rows, w_own, w_other):
    depth, width = w_own.shape
    return pl.pallas_call(
        project_kernel,
        out_shape=pltpu.HBM((GROUPS, ROWS, width + HEAD), jnp.bfloat16),
        in_specs=[whole(pltpu.SMEM), whole(), whole(), whole()],
        out_specs=whole(pltpu.HBM),
        scratch_shapes=[
            pltpu.VMEM((SEQ * GROUPS, 2 * depth), jnp.float32),
            pltpu.VMEM((2 * depth, width), jnp.bfloat16),
            pltpu.VMEM((GROUPS, ROWS, width + HEAD), jnp.bfloat16),
            pltpu.SemaphoreType.DMA((GROUPS,)),
        ],
        compiler_params=pltpu.CompilerParams(vmem_limit_bytes=24 << 20),
        name="project",
    )(place, rows, w_own, w_other)


def rotate_kernel(parts, cos_ref, sin_ref, q_ref, kv_ref, held, sem):
    width = (HEADS + 2) * HEAD
    tail = sum(parts[g, :, width:].astype(jnp.float32) for g in range(GROUPS))
    squares = tail[:, :1] + tail[:, 1:2]
    inv = lax.rsqrt(squares / FEATURES + NORM_EPS)
    cosine, sine = cos_ref[...], sin_ref[...]
    sends = [pltpu.make_async_copy(held, kv_ref.at[m], sem.at[m]) for m in range(SAMP)]
    for h in (HEADS, HEADS + 1, *range(HEADS)):
        columns = pl.ds(h * HEAD, HEAD)
        u = sum(parts[g, :, columns].astype(jnp.float32) for g in range(GROUPS)) * inv
        if h <= HEADS:
            u = u * cosine + pltpu.roll(u, HEAD // 2, 1) * sine
        u = u.astype(jnp.bfloat16)
        if h < HEADS:
            q_ref[pl.ds(h * ROWS, ROWS), :] = u
        else:
            held[:, pl.ds((h - HEADS) * HEAD, HEAD)] = u
        if h == HEADS + 1:
            for send in sends:
                send.start()
    for send in sends:
        send.wait()


def rotate(parts, cosine, sine):
    return pl.pallas_call(
        rotate_kernel,
        out_shape=(
            jax.ShapeDtypeStruct((HEADS * ROWS, HEAD), jnp.bfloat16),
            pltpu.HBM((SAMP, ROWS, 2 * HEAD), jnp.bfloat16),
        ),
        in_specs=[whole()] * 3,
        out_specs=(whole(), whole(pltpu.HBM)),
        scratch_shapes=[
            pltpu.VMEM((ROWS, 2 * HEAD), jnp.bfloat16),
            pltpu.SemaphoreType.DMA((SAMP,)),
        ],
        compiler_params=pltpu.CompilerParams(vmem_limit_bytes=16 << 20),
        name="rotate",
    )(parts, cosine, sine)


def prefix_kernel(count, q_ref, kv_ref, acc_ref, max_ref, sum_ref, *, slots):
    step = pl.program_id(0)

    @pl.when(step == 0)
    def _():
        acc_ref[...] = jnp.zeros_like(acc_ref)
        max_ref[...] = jnp.full_like(max_ref, MASK_FILL)
        sum_ref[...] = jnp.zeros_like(sum_ref)

    first = step * slots

    def absorb(masked):
        keys, values = kv_ref[0, 0], kv_ref[1, 0]
        values = jnp.concatenate([values, jnp.ones_like(values)], axis=1)
        if masked:
            ids = first + lax.broadcasted_iota(jnp.int32, (1, slots), 1)
            bias = jnp.where(ids < count[0], 0.0, MASK_FILL)
        for h in range(HEADS):
            rows = pl.ds(h * ROWS, ROWS)
            scores = lax.dot_general(
                q_ref[rows, :], keys, LAST_DIMS, preferred_element_type=jnp.float32
            )
            if masked:
                scores = scores + bias
            old = max_ref[rows, :]
            new = jnp.maximum(old, jnp.max(scores, axis=1, keepdims=True))
            weights = jnp.exp2((scores - new[:, :1]) * LOG2_SCALE).astype(jnp.bfloat16)
            factor = jnp.exp2((old - new) * LOG2_SCALE)
            both = jnp.dot(weights, values, preferred_element_type=jnp.float32)
            acc_ref[rows, :] = acc_ref[rows, :] * factor + both[:, :HEAD]
            sum_ref[rows, :] = sum_ref[rows, :] * factor + both[:, HEAD:]
            max_ref[rows, :] = new

    @pl.when(first + slots <= count[0])
    def _():
        absorb(False)

    @pl.when((first < count[0]) & (first + slots > count[0]))
    def _():
        absorb(True)


def attend_prefix(count, queries, cache, slots=2048):
    n = queries.shape[0]
    state = jax.ShapeDtypeStruct((n, HEAD), jnp.float32)

    def cache_block(step, count):
        return (0, 0, jnp.minimum(step, lax.div(count[0] - 1, slots)), 0)

    return pl.pallas_call(
        functools.partial(prefix_kernel, slots=slots),
        out_shape=(state, state, state),
        grid_spec=pltpu.PrefetchScalarGridSpec(
            num_scalar_prefetch=1,
            grid=(cache.shape[2] // slots,),
            in_specs=[
                pl.BlockSpec((n, HEAD), lambda step, count: (0, 0)),
                pl.BlockSpec((2, 1, slots, HEAD), cache_block),
            ],
            out_specs=[pl.BlockSpec((n, HEAD), lambda step, count: (0, 0))] * 3,
        ),
        compiler_params=pltpu.CompilerParams(
            dimension_semantics=("arbitrary",), vmem_limit_bytes=24 << 20
        ),
        name="prefix",
    )(count, queries, cache)


def finish_kernel(place, q_ref, acc_ref, max_ref, sum_ref, kv, out, block, comp_block, sem):
    group, core = place[0], place[1]
    keys = jnp.concatenate([kv[m, :PROMPT_ROWS, :HEAD] for m in range(SAMP)], axis=0)
    values = jnp.concatenate([kv[m, :PROMPT_ROWS, HEAD:] for m in range(SAMP)], axis=0)
    values = jnp.concatenate([values, jnp.ones_like(values)], axis=1)
    first = 2 * (group - group % 2) + core
    comp = jnp.concatenate([kv[first, PROMPT_ROWS:, :], kv[first + 2, PROMPT_ROWS:, :]], axis=0)
    comp_values = jnp.concatenate([comp[:, HEAD:], jnp.ones_like(comp[:, HEAD:])], axis=1)
    n = keys.shape[0]
    column = lax.broadcasted_iota(jnp.int32, (1, n), 1)
    samp = column // PROMPT_ROWS
    key_id = 256 * (column // 16 % SEQ) + 128 * (samp % 2) + 16 * (samp // 2) + column % 16
    row = lax.broadcasted_iota(jnp.int32, (ROWS, 1), 0)
    own_id = 256 * (row // 16) + 128 * core + 16 * group + row % 16
    limit = jnp.where(row < PROMPT_ROWS, own_id, n)
    bias = jnp.where(key_id <= limit, 0.0, MASK_FILL)
    column = lax.broadcasted_iota(jnp.int32, (1, 2 * SEQ), 1)
    live = (column % SEQ == row - PROMPT_ROWS) & (column // SEQ <= group % 2)
    comp_bias = jnp.where(live, 0.0, MASK_FILL)
    for h in range(HEADS):
        rows = pl.ds(h * ROWS, ROWS)
        q = q_ref[rows, :]
        scores = lax.dot_general(q, keys, LAST_DIMS, preferred_element_type=jnp.float32) + bias
        comp_scores = (
            lax.dot_general(q, comp[:, :HEAD], LAST_DIMS, preferred_element_type=jnp.float32)
            + comp_bias
        )
        old = max_ref[rows, :]
        new = jnp.maximum(old, jnp.max(scores, axis=1, keepdims=True))
        new = jnp.maximum(new, jnp.max(comp_scores, axis=1, keepdims=True))
        weights = jnp.exp2((scores - new[:, :1]) * LOG2_SCALE).astype(jnp.bfloat16)
        comp_weights = jnp.exp2((comp_scores - new[:, :1]) * LOG2_SCALE).astype(jnp.bfloat16)
        factor = jnp.exp2((old - new) * LOG2_SCALE)
        both = jnp.dot(weights, values, preferred_element_type=jnp.float32)
        both = both + jnp.dot(comp_weights, comp_values, preferred_element_type=jnp.float32)
        context = acc_ref[rows, :] * factor + both[:, :HEAD]
        context = context / (sum_ref[rows, :] * factor + both[:, HEAD:])
        for s in range(SEQ):
            block[s, pl.ds(16 * h, 16), :] = context[16 * s : 16 * s + 16].astype(jnp.bfloat16)
            comp_block[s, pl.ds(h, 1), :] = context[PROMPT_ROWS + s : PROMPT_ROWS + s + 1]
    for s in range(SEQ):
        block[s, PROMPT_ROWS:, :] = comp_block[s].astype(jnp.bfloat16)

    def send(g):
        return pltpu.make_async_copy(block, out.at[:, g], sem.at[g])

    for g in range(GROUPS):
        send(g).start()
    for g in range(GROUPS):
        send(g).wait()


def finish(place, queries, state, kv):
    return pl.pallas_call(
        finish_kernel,
        out_shape=pltpu.HBM((SEQ, GROUPS, ROWS, HEAD), jnp.bfloat16),
        in_specs=[whole(pltpu.SMEM)] + [whole()] * 5,
        out_specs=whole(pltpu.HBM),
        scratch_shapes=[
            pltpu.VMEM((SEQ, ROWS, HEAD), jnp.bfloat16),
            pltpu.VMEM((SEQ, HEADS, HEAD), jnp.float32),
            pltpu.SemaphoreType.DMA((GROUPS,)),
        ],
        compiler_params=pltpu.CompilerParams(vmem_limit_bytes=28 << 20),
        name="finish",
    )(place, queries, *state, kv)


def output_kernel(place, source, kept, came, same, crossed, *refs):
    weights, (prompt_out, comp_out, matrix, sem) = refs[:SEQ], refs[SEQ:]
    loads = [pltpu.make_async_copy(w, matrix.at[j], sem.at[j]) for j, w in enumerate(weights)]
    for load in loads:
        load.start()
    core = place[1]
    blocks = (same, crossed)
    n = SAMP * HEADS
    to_row = lax.broadcasted_iota(jnp.int32, (n, n), 0)
    from_row = lax.broadcasted_iota(jnp.int32, (n, n), 1)
    head, out_row = to_row // SAMP, to_row % SAMP
    crossing = (out_row // GROUPS + core) % 2
    wanted = crossing * (GROUPS * HEADS) + (out_row % GROUPS) * HEADS + head
    order = jnp.where(from_row == wanted, 1.0, 0.0).astype(jnp.bfloat16)
    total = jnp.zeros((SAMP * 17, prompt_out.shape[1]), jnp.float32)
    for j in range(SEQ):
        first = source[j] * GROUPS
        left = []
        for b in blocks:
            for g in range(GROUPS):
                parts = [b[first + g, pl.ds(16 * h, 16), :] for h in range(HEADS)]
                left.append(jnp.concatenate(parts, axis=1))
        comp = [b[first + g, PROMPT_ROWS:, :] for b in blocks for g in range(GROUPS)]
        comp = jnp.concatenate(comp, axis=0)
        comp = jnp.dot(order, comp, preferred_element_type=jnp.float32).astype(jnp.bfloat16)
        parts = [comp[SAMP * h : SAMP * h + SAMP] for h in range(HEADS)]
        left.append(jnp.concatenate(parts, axis=1))
        left = jnp.concatenate(left, axis=0)
        loads[j].wait()
        total = total + jnp.dot(left, matrix[j], preferred_element_type=jnp.float32)
    rests = (kept, came)
    for r in range(2):
        at = pl.ds(pl.multiple_of(((core + r) % 2) * PROMPT_ROWS, PROMPT_ROWS), PROMPT_ROWS)
        rest = rests[r][:PROMPT_ROWS, :].astype(jnp.float32)
        prompt_out[at, :] = (total[PROMPT_ROWS * r : PROMPT_ROWS * (r + 1)] + rest).astype(
            jnp.bfloat16
        )
    low = jnp.concatenate([kept[PROMPT_ROWS:, :], came[PROMPT_ROWS:, :]], axis=0)
    high = jnp.concatenate([came[PROMPT_ROWS:, :], kept[PROMPT_ROWS:, :]], axis=0)
    rest = jnp.where(core == 0, low.astype(jnp.float32), high.astype(jnp.float32))
    comp_out[...] = (total[2 * PROMPT_ROWS :] + rest).astype(jnp.bfloat16)


def output(place, source, kept, came, same, crossed, weights):
    width = kept.shape[1]
    return pl.pallas_call(
        output_kernel,
        out_shape=(
            jax.ShapeDtypeStruct((2 * PROMPT_ROWS, width), jnp.bfloat16),
            jax.ShapeDtypeStruct((SAMP, width), jnp.bfloat16),
        ),
        in_specs=[whole(pltpu.SMEM)] * 2 + [whole()] * 4 + [whole(pl.ANY)] * SEQ,
        out_specs=(whole(), whole()),
        scratch_shapes=[
            pltpu.VMEM((SEQ, HEADS * HEAD, width), jnp.bfloat16),
            pltpu.SemaphoreType.DMA((SEQ,)),
        ],
        compiler_params=pltpu.CompilerParams(vmem_limit_bytes=30 << 20),
        name="output",
    )(place, source, kept, came, same, crossed, *weights)


def body(
    prompt_ids,
    comp_ids,
    prefix_len,
    prompt_offset,
    embed_table,
    attn_gain,
    query_key_value_weight,
    w_out,
    key_value_cache,
):
    seq_index = lax.axis_index("seq")
    samp_index = lax.axis_index("samp")
    group, core = samp_index // 2, samp_index % 2
    place = jnp.stack([group, core]).astype(jnp.int32)
    vocab_rows, width = embed_table.shape

    ids = [prompt_ids.reshape(SEQ, 2, PROMPT_ROWS), comp_ids.reshape(SEQ, 2, GROUPS)]
    ids = jnp.concatenate(ids, axis=2)
    local = jnp.clip(ids.reshape(-1) - seq_index * vocab_rows, 0, vocab_rows - 1)
    picked = embed_table.at[local].get(mode="promise_in_bounds").reshape(2 * SEQ, ROWS, width)
    got = exchange(picked, ("seq", "samp"), SEQ_CORE)
    own_ids = lax.dynamic_index_in_dim(ids.reshape(-1, ROWS), 2 * seq_index + core, 0, keepdims=False)
    copies, kept, given = merge(place, got, (own_ids // vocab_rows)[:, None])

    scaled = query_key_value_weight.astype(jnp.float32) * attn_gain.astype(jnp.float32)[:, None]
    scaled = scaled.astype(jnp.bfloat16)
    scaled_other = to_other_core(scaled)
    out_flip = to_seq(w_out, (0, 1))

    rows = exchange(copies, "seq")
    came = to_other_core(given)
    partial = project(place, rows, scaled, scaled_other)
    parts = exchange(partial, "samp", SAME_CORE)

    w_own, w_flip, _ = lax.optimization_barrier((w_out, out_flip, rows))
    w_next, w_last = to_seq(w_own, (3, 0)), to_seq(w_own, (1, 0))
    w_flip, w_next, w_last = lax.optimization_barrier((w_flip, w_next, w_last))
    w_next_flip, w_last_flip = to_seq(w_flip, (3, 0)), to_seq(w_flip, (1, 0))
    w_far = to_seq(w_next, (3, 0))

    row = jnp.arange(ROWS, dtype=jnp.int32)
    own_prompt = 256 * (row // 16) + 128 * core + 16 * group + row % 16
    position = jnp.where(row < PROMPT_ROWS, own_prompt, 2048 + group % 2) + prompt_offset[0]
    angles = position.astype(jnp.float32)[:, None] * rope_freqs(HEAD)[None, :]
    cosine, sine = jnp.cos(angles), jnp.sin(angles)
    cosine = jnp.concatenate([cosine, cosine], axis=1)
    sine = jnp.concatenate([-sine, sine], axis=1)
    queries, kv = rotate(parts, cosine, sine)
    all_kv = exchange(kv, "samp")
    queries, w_last_flip = lax.optimization_barrier((queries, w_last_flip))
    w_far_flip = to_seq(w_last_flip, (1, 0))
    state = attend_prefix(prefix_len, queries, key_value_cache)
    weights = [w_own, w_flip, w_next, w_next_flip, w_last, w_last_flip, w_far, w_far_flip]
    context = finish(place, queries, state, all_kv).reshape(SEQ * GROUPS, ROWS, HEAD)

    same = exchange(context, ("seq", "samp"), SEQ_GROUP)
    crossed = to_other_core(same)
    source = jnp.stack([moved(seq_index, shift) for shift in SHIFTS]).astype(jnp.int32)
    prompt_out, comp_out = output(place, source, kept, came, same, crossed, weights)
    return prompt_out, comp_out.reshape(8, 2, width)


def solution(mesh):
    placed = (
        P(),
        P(),
        P(),
        P(),
        P("seq", "samp"),
        P("samp"),
        P("samp", "seq"),
        P("seq", "samp"),
        P(None, "seq", None, None),
    )
    return jax.shard_map(
        body,
        mesh=mesh,
        in_specs=placed,
        out_specs=(P("seq", "samp"), P("seq", None, "samp")),
        check_vma=False,
    )
```

```python
import functools
import math

import jax
import jax.numpy as jnp
from jax import lax
from jax.experimental import pallas as pl
from jax.experimental.pallas import tpu as pltpu
from jax.sharding import PartitionSpec as P


NORM_EPS = 1e-05
MASK_FILL = -1e30
HEAD = 128
HEADS = 8
SEQ = 8
GROUPS = 8
SAMP = 16
ROWS = 136
PROMPT_ROWS = 128
FEATURES = 8192
LOG2_SCALE = math.log2(math.e) / math.sqrt(HEAD)
LAST_DIMS = (((1,), (1,)), ((), ()))

SLOTS = 8
TILES = 4
SEQ_SLOT = [[SAMP * s + 8 * pair + f for s in range(SEQ) for f in range(SLOTS)] for pair in range(2)]
SAME_PAIR = [[8 * pair + f for f in range(SLOTS)] for pair in range(2)]
SEQ_GROUP = [[SAMP * s + 2 * g + c for s in range(SEQ) for g in range(GROUPS)] for c in range(2)]
SHIFTS = ((0, 0), (0, 1), (1, 0), (1, 1), (3, 0), (3, 1), (2, 0), (2, 1))


def rope_freqs(head_dim):
    half_dim = head_dim // 2
    dim_index = jnp.arange(half_dim, dtype=jnp.float32)
    base_freq = 1.0 / jnp.power(500000.0, 2.0 * dim_index / head_dim)
    wavelength = 2.0 * math.pi / base_freq
    blend = (8192.0 / wavelength - 1.0) / 3.0
    middle = (1.0 - blend) * base_freq / 8.0 + blend * base_freq
    return jnp.where(
        wavelength > 8192.0, base_freq / 8.0, jnp.where(wavelength < 2048.0, base_freq, middle)
    )


def moved(index, shift, sign=1):
    return (index % 4 + sign * shift[0] + 4) % 4 + 4 * ((index // 4) ^ shift[1])


def to_seq(block, shift):
    return lax.ppermute(block, "seq", [(i, moved(i, shift)) for i in range(SEQ)])


def to_other_core(block):
    return lax.ppermute(block, "samp", [(i, i ^ 1) for i in range(SAMP)])


def to_ring(block, step):
    pairs = [(m, m // 8 * 8 + (m % 8 + 2 * step) % 8) for m in range(SAMP)]
    return lax.ppermute(block, "samp", pairs)


def to_other_pair(block):
    return lax.ppermute(block, "samp", [(m, (m + 8) % SAMP) for m in range(SAMP)])


def exchange(blocks, axes, groups=None):
    return lax.all_to_all(blocks, axes, 0, 0, tiled=True, axis_index_groups=groups)


def whole(memory_space=pltpu.VMEM):
    return pl.BlockSpec(memory_space=memory_space)


def selection(rows, columns, wanted):
    row = lax.broadcasted_iota(jnp.int32, (rows, columns), 0)
    column = lax.broadcasted_iota(jnp.int32, (rows, columns), 1)
    return jnp.where(column == wanted(row), 1.0, 0.0).astype(jnp.bfloat16)


def selected(matrix, block):
    return jnp.dot(matrix, block, preferred_element_type=jnp.float32)


def arrange_kernel(picked, out, comp, sem):
    n = SEQ * SLOTS
    sends = [
        pltpu.make_async_copy(
            picked.at[pl.ds(0, n), :, pl.ds(HEAD * k, HEAD)], out.at[:, pl.ds(32 * k, 32), :], sem.at[k]
        )
        for k in range(TILES)
    ]
    for send in sends:
        send.start()
    rows = jnp.concatenate([picked[n + i] for i in range(4)], axis=0)
    total = jnp.zeros((8 * n, HEAD), jnp.float32)
    for k in range(TILES):
        matrix = selection(
            8 * n, 2 * n, lambda r: jnp.where(r // 2 % TILES == k, r // 8 * 2 + r % 2, -1)
        )
        total = total + selected(matrix, rows[:, HEAD * k : HEAD * k + HEAD])
    comp[...] = total.astype(jnp.bfloat16).reshape(n, 8, HEAD)
    last = pltpu.make_async_copy(comp, out.at[:, pl.ds(PROMPT_ROWS, 8), :], sem.at[TILES])
    last.start()
    for send in sends + [last]:
        send.wait()


def arrange(picked):
    n = SEQ * SLOTS
    return pl.pallas_call(
        arrange_kernel,
        out_shape=pltpu.HBM((n, ROWS, HEAD), jnp.bfloat16),
        in_specs=[whole()],
        out_specs=whole(pltpu.HBM),
        scratch_shapes=[
            pltpu.VMEM((n, 8, HEAD), jnp.bfloat16),
            pltpu.SemaphoreType.DMA((TILES + 1,)),
        ],
        compiler_params=pltpu.CompilerParams(vmem_limit_bytes=16 << 20),
        name="arrange",
    )(picked)


def merge_kernel(got, owner, copies, merged, held, sem):
    sends = [pltpu.make_async_copy(held, copies.at[s], sem.at[s]) for s in range(SEQ)]
    sends.append(pltpu.make_async_copy(held, merged, sem.at[SEQ]))
    owns = [owner[...] == s for s in range(SEQ)]
    for f in range(SLOTS):
        total = jnp.zeros((ROWS, HEAD), jnp.float32)
        for s in range(SEQ):
            total = jnp.where(owns[s], got[SLOTS * s + f].astype(jnp.float32), total)
        held[f] = total.astype(jnp.bfloat16)
    for send in sends:
        send.start()
    for send in sends:
        send.wait()


def merge(got, owner):
    return pl.pallas_call(
        merge_kernel,
        out_shape=(
            pltpu.HBM((SEQ, SLOTS, ROWS, HEAD), jnp.bfloat16),
            pltpu.HBM((SLOTS, ROWS, HEAD), jnp.bfloat16),
        ),
        in_specs=[whole(), whole()],
        out_specs=(whole(pltpu.HBM), whole(pltpu.HBM)),
        scratch_shapes=[
            pltpu.VMEM((SLOTS, ROWS, HEAD), jnp.bfloat16),
            pltpu.SemaphoreType.DMA((SEQ + 1,)),
        ],
        compiler_params=pltpu.CompilerParams(vmem_limit_bytes=16 << 20),
        name="merge",
    )(got, owner)


def project_kernel(rows, *refs):
    weights, (kept, sent, matrix, total, own, other, sem) = refs[:SLOTS], refs[SLOTS:]
    loads = [pltpu.make_async_copy(w, matrix.at[j], sem.at[j]) for j, w in enumerate(weights)]
    for load in loads:
        load.start()
    samp = lax.axis_index("samp")
    pair, slot = samp // 8, samp % 8
    slots = [(slot // 2 + step) % 4 * 2 + (slot + cross) % 2 for cross in (0, 1) for step in (0, 1, 3, 2)]
    n = 8 * SEQ
    orders = [
        selection(
            2 * SEQ, n, lambda r: r % SEQ * 8 + 2 * k + jnp.where(pair == 0, r // SEQ, 1 - r // SEQ)
        )
        for k in range(TILES)
    ]
    squares = jnp.zeros((2 * ROWS, 1), jnp.float32)
    for j in range(SLOTS):
        f = slots[j]
        comp = jnp.concatenate([rows[s, f, PROMPT_ROWS:, :] for s in range(SEQ)], axis=0)
        comp = [selected(order, comp).astype(jnp.bfloat16) for order in orders]
        comp = jnp.concatenate(comp, axis=1)
        parts = []
        for r in range(2):
            first = 16 * ((pair + r) % 2)
            for s in range(SEQ):
                tiles = [
                    rows[s, f, pl.ds(pl.multiple_of(32 * k + first, 16), 16), :] for k in range(TILES)
                ]
                parts.append(jnp.concatenate(tiles, axis=1))
            parts.append(comp[SEQ * r : SEQ * r + SEQ])
        block = jnp.concatenate(parts, axis=0)
        wide = block.astype(jnp.float32)
        squares = squares + jnp.sum(wide * wide, axis=1, keepdims=True)
        loads[j].wait()
        product = jnp.dot(block, matrix[j], preferred_element_type=jnp.float32)
        if j == 0:
            total[...] = product
        elif j < SLOTS - 1:
            total[...] += product
        else:
            product = total[...] + product
    high = squares.astype(jnp.bfloat16).astype(jnp.float32)
    lane = lax.broadcasted_iota(jnp.int32, (2 * ROWS, HEAD), 1)
    extra = jnp.where(lane == 0, high, jnp.where(lane == 1, squares - high, 0.0))
    width = product.shape[1]
    for r, out in enumerate((own, other)):
        out[:, :width] = product[ROWS * r : ROWS * r + ROWS].astype(jnp.bfloat16)
        out[:, width:] = extra[ROWS * r : ROWS * r + ROWS].astype(jnp.bfloat16)
    sends = [
        pltpu.make_async_copy(other, sent, sem.at[SLOTS]),
        pltpu.make_async_copy(own, kept, sem.at[SLOTS + 1]),
    ]
    for send in sends:
        send.start()
    for send in sends:
        send.wait()


def project(rows, weights):
    depth, width = weights[0].shape
    shape = (ROWS, width + HEAD)
    return pl.pallas_call(
        project_kernel,
        out_shape=(pltpu.HBM(shape, jnp.bfloat16), pltpu.HBM(shape, jnp.bfloat16)),
        in_specs=[whole()] + [whole(pl.ANY)] * SLOTS,
        out_specs=(whole(pltpu.HBM), whole(pltpu.HBM)),
        scratch_shapes=[
            pltpu.VMEM((SLOTS, depth, width), jnp.bfloat16),
            pltpu.VMEM((2 * ROWS, width), jnp.float32),
            pltpu.VMEM(shape, jnp.bfloat16),
            pltpu.VMEM(shape, jnp.bfloat16),
            pltpu.SemaphoreType.DMA((SLOTS + 2,)),
        ],
        compiler_params=pltpu.CompilerParams(vmem_limit_bytes=28 << 20),
        name="project",
    )(rows, *weights)


def rotate_kernel(kept, given, cos_ref, sin_ref, q_ref, kv_ref, held, mine, sem):
    load = pltpu.make_async_copy(kept, mine, sem.at[SAMP])
    load.start()
    load.wait()
    width = (HEADS + 2) * HEAD
    tail = sum(p[:, width:].astype(jnp.float32) for p in (mine, given))
    squares = tail[:, :1] + tail[:, 1:2]
    inv = lax.rsqrt(squares / FEATURES + NORM_EPS)
    cosine, sine = cos_ref[...], sin_ref[...]
    sends = [pltpu.make_async_copy(held, kv_ref.at[m], sem.at[m]) for m in range(SAMP)]
    for h in (HEADS, HEADS + 1, *range(HEADS)):
        columns = pl.ds(h * HEAD, HEAD)
        u = sum(p[:, columns].astype(jnp.float32) for p in (mine, given)) * inv
        if h <= HEADS:
            u = u * cosine + pltpu.roll(u, HEAD // 2, 1) * sine
        if h < HEADS:
            u = u * LOG2_SCALE
        u = u.astype(jnp.bfloat16)
        if h < HEADS:
            q_ref[pl.ds(h * ROWS, ROWS), :] = u
        else:
            held[:, pl.ds((h - HEADS) * HEAD, HEAD)] = u
        if h == HEADS + 1:
            for send in sends:
                send.start()
    for send in sends:
        send.wait()


def rotate(mine, given, cosine, sine):
    return pl.pallas_call(
        rotate_kernel,
        out_shape=(
            jax.ShapeDtypeStruct((HEADS * ROWS, HEAD), jnp.bfloat16),
            pltpu.HBM((SAMP, ROWS, 2 * HEAD), jnp.bfloat16),
        ),
        in_specs=[whole(pl.ANY)] + [whole()] * 3,
        out_specs=(whole(), whole(pltpu.HBM)),
        scratch_shapes=[
            pltpu.VMEM((ROWS, 2 * HEAD), jnp.bfloat16),
            pltpu.VMEM(mine.shape, jnp.bfloat16),
            pltpu.SemaphoreType.DMA((SAMP + 1,)),
        ],
        compiler_params=pltpu.CompilerParams(vmem_limit_bytes=16 << 20),
        name="rotate",
    )(mine, given, cosine, sine)


def prefix_kernel(count, q_ref, kv_ref, acc_ref, max_ref, sum_ref, token_ref, *, slots):
    step = pl.program_id(0)

    @pl.when(step == 0)
    def _():
        acc_ref[...] = jnp.zeros_like(acc_ref)
        max_ref[...] = jnp.full_like(max_ref, MASK_FILL)
        sum_ref[...] = jnp.zeros_like(sum_ref)
        token_ref[...] = jnp.zeros_like(token_ref)

    first = step * slots

    def absorb(masked):
        keys, values = kv_ref[0, 0], kv_ref[1, 0]
        values = jnp.concatenate([values, jnp.ones_like(values)], axis=1)
        if masked:
            ids = first + lax.broadcasted_iota(jnp.int32, (1, slots), 1)
            bias = jnp.where(ids < count[0], 0.0, MASK_FILL)
        for h in range(HEADS):
            rows = pl.ds(h * ROWS, ROWS)
            scores = lax.dot_general(
                q_ref[rows, :], keys, LAST_DIMS, preferred_element_type=jnp.float32
            )
            if masked:
                scores = scores + bias
            old = max_ref[rows, :]
            new = jnp.maximum(old, jnp.max(scores, axis=1, keepdims=True))
            weights = jnp.exp2(scores - new[:, :1]).astype(jnp.bfloat16)
            factor = jnp.exp2(old - new)
            both = jnp.dot(weights, values, preferred_element_type=jnp.float32)
            acc_ref[rows, :] = acc_ref[rows, :] * factor + both[:, :HEAD]
            sum_ref[rows, :] = sum_ref[rows, :] * factor + both[:, HEAD:]
            max_ref[rows, :] = new

    @pl.when(first + slots <= count[0])
    def _():
        absorb(False)

    @pl.when((first < count[0]) & (first + slots > count[0]))
    def _():
        absorb(True)


def attend_prefix(count, queries, cache, slots=2048):
    n = queries.shape[0]
    state = jax.ShapeDtypeStruct((n, HEAD), jnp.float32)

    def cache_block(step, count):
        return (0, 0, jnp.minimum(step, lax.div(count[0] - 1, slots)), 0)

    return pl.pallas_call(
        functools.partial(prefix_kernel, slots=slots),
        out_shape=(state, state, state, jax.ShapeDtypeStruct((8, HEAD), jnp.float32)),
        grid_spec=pltpu.PrefetchScalarGridSpec(
            num_scalar_prefetch=1,
            grid=(cache.shape[2] // slots,),
            in_specs=[
                pl.BlockSpec((n, HEAD), lambda step, count: (0, 0)),
                pl.BlockSpec((2, 1, slots, HEAD), cache_block),
            ],
            out_specs=[pl.BlockSpec((n, HEAD), lambda step, count: (0, 0))] * 3
            + [pl.BlockSpec((8, HEAD), lambda step, count: (0, 0))],
        ),
        compiler_params=pltpu.CompilerParams(
            dimension_semantics=("arbitrary",), vmem_limit_bytes=14 << 20
        ),
        name="prefix",
    )(count, queries, cache)


def finish_kernel(q_ref, acc_ref, max_ref, sum_ref, kv, out, block, comp_block, sem):
    samp_index = lax.axis_index("samp")
    pair, slot = samp_index // 8, samp_index % 8
    keys = jnp.concatenate([kv[m, :PROMPT_ROWS, :HEAD] for m in range(SAMP)], axis=0)
    values = jnp.concatenate([kv[m, :PROMPT_ROWS, HEAD:] for m in range(SAMP)], axis=0)
    values = jnp.concatenate([values, jnp.ones_like(values)], axis=1)
    comp = jnp.concatenate([kv[slot + 8 * r, PROMPT_ROWS:, :] for r in range(2)], axis=0)
    comp_values = jnp.concatenate([comp[:, HEAD:], jnp.ones_like(comp[:, HEAD:])], axis=1)
    n = keys.shape[0]
    column = lax.broadcasted_iota(jnp.int32, (1, n), 1)
    samp = column // PROMPT_ROWS
    key_id = 256 * (column // 16 % SEQ) + 32 * (samp % 8) + 16 * (samp // 8) + column % 16
    row = lax.broadcasted_iota(jnp.int32, (ROWS, 1), 0)
    own_id = 256 * (row // 16) + 32 * slot + 16 * pair + row % 16
    limit = jnp.where(row < PROMPT_ROWS, own_id, n)
    bias = jnp.where(key_id <= limit, 0.0, MASK_FILL)
    column = lax.broadcasted_iota(jnp.int32, (1, 2 * SEQ), 1)
    live = (column % SEQ == row - PROMPT_ROWS) & (column // SEQ <= pair)
    comp_bias = jnp.where(live, 0.0, MASK_FILL)
    for h in range(HEADS):
        rows = pl.ds(h * ROWS, ROWS)
        q = q_ref[rows, :]
        scores = lax.dot_general(q, keys, LAST_DIMS, preferred_element_type=jnp.float32) + bias
        comp_scores = (
            lax.dot_general(q, comp[:, :HEAD], LAST_DIMS, preferred_element_type=jnp.float32)
            + comp_bias
        )
        old = max_ref[rows, :]
        new = jnp.maximum(old, jnp.max(scores, axis=1, keepdims=True))
        new = jnp.maximum(new, jnp.max(comp_scores, axis=1, keepdims=True))
        weights = jnp.exp2(scores - new[:, :1]).astype(jnp.bfloat16)
        comp_weights = jnp.exp2(comp_scores - new[:, :1]).astype(jnp.bfloat16)
        factor = jnp.exp2(old - new)
        both = jnp.dot(weights, values, preferred_element_type=jnp.float32)
        both = both + jnp.dot(comp_weights, comp_values, preferred_element_type=jnp.float32)
        context = acc_ref[rows, :] * factor + both[:, :HEAD]
        context = context / (sum_ref[rows, :] * factor + both[:, HEAD:])
        for s in range(SEQ):
            block[s, pl.ds(16 * h, 16), :] = context[16 * s : 16 * s + 16].astype(jnp.bfloat16)
            comp_block[s, pl.ds(h, 1), :] = context[PROMPT_ROWS + s : PROMPT_ROWS + s + 1]
    for s in range(SEQ):
        block[s, PROMPT_ROWS:, :] = comp_block[s].astype(jnp.bfloat16)

    def send(g):
        return pltpu.make_async_copy(block, out.at[:, g], sem.at[g])

    for g in range(GROUPS):
        send(g).start()
    for g in range(GROUPS):
        send(g).wait()


def finish(queries, state, kv):
    return pl.pallas_call(
        finish_kernel,
        out_shape=pltpu.HBM((SEQ, GROUPS, ROWS, HEAD), jnp.bfloat16),
        in_specs=[whole()] * 5,
        out_specs=whole(pltpu.HBM),
        scratch_shapes=[
            pltpu.VMEM((SEQ, ROWS, HEAD), jnp.bfloat16),
            pltpu.VMEM((SEQ, HEADS, HEAD), jnp.float32),
            pltpu.SemaphoreType.DMA((GROUPS,)),
        ],
        compiler_params=pltpu.CompilerParams(vmem_limit_bytes=14 << 20),
        name="finish",
    )(queries, *state, kv)


def output_kernel(rest, same, crossed, *refs):
    weights, (prompt_out, comp_out, matrix, sem) = refs[:SEQ], refs[SEQ:]
    loads = [pltpu.make_async_copy(w, matrix.at[j], sem.at[j]) for j, w in enumerate(weights)]
    for load in loads:
        load.start()
    core = lax.axis_index("samp") % 2
    seq = lax.axis_index("seq")
    blocks = (same, crossed)
    n = SAMP * HEADS

    def comp_source(r):
        head, token = r // SAMP, r % SAMP
        group = token % 2 * 4 + token // 4
        crossing = (token // 2 + core) % 2
        return (crossing * GROUPS + group) * HEADS + head

    order = selection(n, n, comp_source)
    total = jnp.zeros((SAMP * 17, matrix.shape[2]), jnp.float32)
    for j in range(SEQ):
        first = moved(seq, SHIFTS[j]) * GROUPS
        left = []
        for b in blocks:
            for g in range(GROUPS):
                parts = [b[first + g, pl.ds(16 * h, 16), :] for h in range(HEADS)]
                left.append(jnp.concatenate(parts, axis=1))
        comp = [b[first + g, PROMPT_ROWS:, :] for b in blocks for g in range(GROUPS)]
        comp = selected(order, jnp.concatenate(comp, axis=0)).astype(jnp.bfloat16)
        parts = [comp[SAMP * h : SAMP * h + SAMP] for h in range(HEADS)]
        left.append(jnp.concatenate(parts, axis=1))
        left = jnp.concatenate(left, axis=0)
        loads[j].wait()
        total = total + jnp.dot(left, matrix[j], preferred_element_type=jnp.float32)
    for r in range(2):
        for g in range(GROUPS):
            slot = 2 * (g % 4) + (core + r) % 2
            at = pl.multiple_of(32 * slot + 16 * (g // 4), 16)
            parts = [
                rest[slot, pl.ds(32 * k + 16 * (g // 4), 16), :].astype(jnp.float32)
                for k in range(TILES)
            ]
            i = 16 * (GROUPS * r + g)
            prompt_out[pl.ds(at, 16), :] = (
                total[i : i + 16] + jnp.concatenate(parts, axis=1)
            ).astype(jnp.bfloat16)
    comp = jnp.concatenate([rest[f, PROMPT_ROWS:, :] for f in range(SLOTS)], axis=0)
    parts = [
        selected(selection(SAMP, 8 * SLOTS, lambda r: r // 2 * 8 + 2 * k + r % 2), comp)
        for k in range(TILES)
    ]
    last = (total[2 * PROMPT_ROWS :] + jnp.concatenate(parts, axis=1)).astype(jnp.bfloat16)
    comp_out[...] = last.reshape(comp_out.shape)


def output(rest, same, crossed, weights):
    width = weights[0].shape[1]
    return pl.pallas_call(
        output_kernel,
        out_shape=(
            jax.ShapeDtypeStruct((2 * PROMPT_ROWS, width), jnp.bfloat16),
            jax.ShapeDtypeStruct((SAMP // 2, 2, width), jnp.bfloat16),
        ),
        in_specs=[whole()] * 3 + [whole(pl.ANY)] * SEQ,
        out_specs=(whole(), whole()),
        scratch_shapes=[
            pltpu.VMEM((SEQ, HEADS * HEAD, width), jnp.bfloat16),
            pltpu.SemaphoreType.DMA((SEQ,)),
        ],
        compiler_params=pltpu.CompilerParams(vmem_limit_bytes=30 << 20),
        name="output",
    )(rest, same, crossed, *weights)


def body(
    prompt_ids,
    comp_ids,
    prefix_len,
    prompt_offset,
    embed_table,
    attn_gain,
    query_key_value_weight,
    w_out,
    key_value_cache,
):
    seq_index = lax.axis_index("seq")
    samp_index = lax.axis_index("samp")
    pair, slot = samp_index // 8, samp_index % 8
    vocab_rows, width = embed_table.shape

    scaled = query_key_value_weight.astype(jnp.float32) * attn_gain.astype(jnp.float32)[:, None]
    scaled = scaled.astype(jnp.bfloat16)
    out_flip = to_seq(w_out, (0, 1))
    w_next, w_last = to_seq(w_out, (3, 0)), to_seq(w_out, (1, 0))
    scaled_next, scaled_last = to_ring(scaled, 3), to_ring(scaled, 1)

    ids = jnp.concatenate([prompt_ids, comp_ids.reshape(-1)])
    local = jnp.clip(ids - seq_index * vocab_rows, 0, vocab_rows - 1)
    picked = embed_table.at[local].get(mode="promise_in_bounds")
    pieces = arrange(picked.reshape(-1, 32, width))
    got = exchange(pieces, ("seq", "samp"), SEQ_SLOT)
    piece_at = SLOTS * seq_index + slot
    own_prompt_ids = lax.dynamic_slice_in_dim(prompt_ids, 32 * piece_at, 32, 0)
    own_comp_ids = lax.dynamic_slice_in_dim(comp_ids.reshape(-1), 2 * piece_at, 2, 0)
    own_ids = jnp.concatenate([jnp.tile(own_prompt_ids, TILES), jnp.tile(own_comp_ids, TILES)])
    owner = (own_ids // vocab_rows)[:, None]
    copies, merged = merge(got, owner)

    rows = exchange(copies, "seq")
    by_ring, _ = lax.optimization_barrier((scaled, copies))
    scaled_far = to_ring(by_ring, 2)
    scales = [scaled, scaled_next, scaled_last, scaled_far]
    scales = scales + [to_other_core(w) for w in scales]
    mine, sent = project(rows, scales)
    given = to_other_pair(sent)
    rest = exchange(merged, "samp", SAME_PAIR)
    given, rest = lax.optimization_barrier((given, rest))

    w_flip, w_last, _ = lax.optimization_barrier((out_flip, w_last, sent))
    w_next_flip, w_last_flip = to_seq(w_flip, (3, 0)), to_seq(w_flip, (1, 0))
    w_far = to_seq(w_last, (1, 0))

    row = jnp.arange(ROWS, dtype=jnp.int32)
    own_prompt = 256 * (row // 16) + 32 * slot + 16 * pair + row % 16
    position = jnp.where(row < PROMPT_ROWS, own_prompt, 2048 + pair) + prompt_offset[0]
    angles = position.astype(jnp.float32)[:, None] * rope_freqs(HEAD)[None, :]
    cosine, sine = jnp.cos(angles), jnp.sin(angles)
    cosine = jnp.concatenate([cosine, cosine], axis=1)
    sine = jnp.concatenate([-sine, sine], axis=1)
    queries, kv = rotate(mine, given, cosine, sine)
    all_kv = exchange(kv, "samp")
    *state, attended = attend_prefix(
        prefix_len, queries, pltpu.with_memory_space_constraint(key_value_cache, pltpu.HBM)
    )
    w_next_flip, _ = lax.optimization_barrier((w_next_flip, attended))
    w_far_flip = to_seq(w_next_flip, (3, 0))
    weights = [w_out, w_flip, w_next, w_next_flip, w_last, w_last_flip, w_far, w_far_flip]
    context = finish(queries, state, all_kv)
    context = context.reshape(SEQ * GROUPS, ROWS, HEAD)

    same = exchange(context, ("seq", "samp"), SEQ_GROUP)
    crossed = to_other_core(same)
    prompt_out, comp_out = output(rest, same, crossed, weights)
    return prompt_out, comp_out


def solution(mesh):
    placed = (
        P(),
        P(),
        P(),
        P(),
        P("seq", "samp"),
        P("samp"),
        P("samp", "seq"),
        P("seq", "samp"),
        P(None, "seq", None, None),
    )
    return jax.shard_map(
        body,
        mesh=mesh,
        in_specs=placed,
        out_specs=(P("seq", "samp"), P("seq", None, "samp")),
        check_vma=False,
    )
```

```python
import functools
import math

import jax
import jax.numpy as jnp
from jax import lax
from jax.experimental import pallas as pl
from jax.experimental.pallas import tpu as pltpu
from jax.sharding import PartitionSpec as P


NORM_EPS = 1e-05
MASK_FILL = -1e30
HEAD = 128
HEADS = 8
SEQ = 8
GROUPS = 8
SAMP = 16
ROWS = 136
PROMPT_ROWS = 128
FEATURES = 8192
LOG2_SCALE = math.log2(math.e) / math.sqrt(HEAD)
LAST_DIMS = (((1,), (1,)), ((), ()))

SLOTS = 8
TILES = 4
SEQ_SLOT = [[SAMP * s + 8 * pair + f for s in range(SEQ) for f in range(SLOTS)] for pair in range(2)]
SAME_PAIR = [[8 * pair + f for f in range(SLOTS)] for pair in range(2)]
SEQ_GROUP = [[SAMP * s + 2 * g + c for s in range(SEQ) for g in range(GROUPS)] for c in range(2)]
SHIFTS = ((0, 0), (0, 1), (1, 0), (1, 1), (3, 0), (3, 1), (2, 0), (2, 1))


def rope_freqs(head_dim):
    half_dim = head_dim // 2
    dim_index = jnp.arange(half_dim, dtype=jnp.float32)
    base_freq = 1.0 / jnp.power(500000.0, 2.0 * dim_index / head_dim)
    wavelength = 2.0 * math.pi / base_freq
    blend = (8192.0 / wavelength - 1.0) / 3.0
    middle = (1.0 - blend) * base_freq / 8.0 + blend * base_freq
    return jnp.where(
        wavelength > 8192.0, base_freq / 8.0, jnp.where(wavelength < 2048.0, base_freq, middle)
    )


def moved(index, shift, sign=1):
    return (index % 4 + sign * shift[0] + 4) % 4 + 4 * ((index // 4) ^ shift[1])


def to_seq(block, shift):
    return lax.ppermute(block, "seq", [(i, moved(i, shift)) for i in range(SEQ)])


def to_other_core(block):
    return lax.ppermute(block, "samp", [(i, i ^ 1) for i in range(SAMP)])


def to_ring(block, step):
    pairs = [(m, m // 8 * 8 + (m % 8 + 2 * step) % 8) for m in range(SAMP)]
    return lax.ppermute(block, "samp", pairs)


def to_other_pair(block):
    return lax.ppermute(block, "samp", [(m, (m + 8) % SAMP) for m in range(SAMP)])


def exchange(blocks, axes, groups=None):
    return lax.all_to_all(blocks, axes, 0, 0, tiled=True, axis_index_groups=groups)


def whole(memory_space=pltpu.VMEM):
    return pl.BlockSpec(memory_space=memory_space)


def in_hbm(block):
    return pltpu.with_memory_space_constraint(block, pltpu.HBM)


def selection(rows, columns, wanted):
    row = lax.broadcasted_iota(jnp.int32, (rows, columns), 0)
    column = lax.broadcasted_iota(jnp.int32, (rows, columns), 1)
    return jnp.where(column == wanted(row), 1.0, 0.0).astype(jnp.bfloat16)


def selected(matrix, block):
    return jnp.dot(matrix, block, preferred_element_type=jnp.float32)


def arrange_kernel(picked, out, comp, sem):
    n = SEQ * SLOTS
    sends = [
        pltpu.make_async_copy(
            picked.at[pl.ds(0, n), :, pl.ds(HEAD * k, HEAD)], out.at[:, pl.ds(32 * k, 32), :], sem.at[k]
        )
        for k in range(TILES)
    ]
    for send in sends:
        send.start()
    rows = jnp.concatenate([picked[n + i] for i in range(4)], axis=0)
    total = jnp.zeros((8 * n, HEAD), jnp.float32)
    for k in range(TILES):
        matrix = selection(
            8 * n, 2 * n, lambda r: jnp.where(r // 2 % TILES == k, r // 8 * 2 + r % 2, -1)
        )
        total = total + selected(matrix, rows[:, HEAD * k : HEAD * k + HEAD])
    comp[...] = total.astype(jnp.bfloat16).reshape(n, 8, HEAD)
    last = pltpu.make_async_copy(comp, out.at[:, pl.ds(PROMPT_ROWS, 8), :], sem.at[TILES])
    last.start()
    for send in sends + [last]:
        send.wait()


def arrange(picked):
    n = SEQ * SLOTS
    return pl.pallas_call(
        arrange_kernel,
        out_shape=pltpu.HBM((n, ROWS, HEAD), jnp.bfloat16),
        in_specs=[whole()],
        out_specs=whole(pltpu.HBM),
        scratch_shapes=[
            pltpu.VMEM((n, 8, HEAD), jnp.bfloat16),
            pltpu.SemaphoreType.DMA((TILES + 1,)),
        ],
        compiler_params=pltpu.CompilerParams(vmem_limit_bytes=16 << 20),
        name="arrange",
    )(picked)


def merge_kernel(got, owners, copies, merged, held, owner, sem):
    load = pltpu.make_async_copy(owners, owner, sem.at[SEQ + 1])
    load.start()
    load.wait()
    sends = [pltpu.make_async_copy(held, copies.at[s], sem.at[s]) for s in range(SEQ)]
    sends.append(pltpu.make_async_copy(held, merged, sem.at[SEQ]))
    owns = [owner[...] == s for s in range(SEQ)]
    for f in range(SLOTS):
        total = jnp.zeros((ROWS, HEAD), jnp.float32)
        for s in range(SEQ):
            total = jnp.where(owns[s], got[SLOTS * s + f].astype(jnp.float32), total)
        held[f] = total.astype(jnp.bfloat16)
    for send in sends:
        send.start()
    for send in sends:
        send.wait()


def merge(got, owner):
    return pl.pallas_call(
        merge_kernel,
        out_shape=(
            pltpu.HBM((SEQ, SLOTS, ROWS, HEAD), jnp.bfloat16),
            pltpu.HBM((SLOTS, ROWS, HEAD), jnp.bfloat16),
        ),
        in_specs=[whole(), whole(pl.ANY)],
        out_specs=(whole(pltpu.HBM), whole(pltpu.HBM)),
        scratch_shapes=[
            pltpu.VMEM((SLOTS, ROWS, HEAD), jnp.bfloat16),
            pltpu.VMEM((ROWS, 1), jnp.int32),
            pltpu.SemaphoreType.DMA((SEQ + 2,)),
        ],
        compiler_params=pltpu.CompilerParams(vmem_limit_bytes=16 << 20),
        name="merge",
    )(got, in_hbm(owner))


def project_kernel(rows, *refs):
    weights, (kept, sent, matrix, total, own, other, sem) = refs[:SLOTS], refs[SLOTS:]
    loads = [pltpu.make_async_copy(w, matrix.at[j], sem.at[j]) for j, w in enumerate(weights)]
    for load in loads:
        load.start()
    samp = lax.axis_index("samp")
    pair, slot = samp // 8, samp % 8
    slots = [(slot // 2 + step) % 4 * 2 + (slot + cross) % 2 for cross in (0, 1) for step in (0, 1, 3, 2)]
    n = 8 * SEQ
    orders = [
        selection(
            2 * SEQ, n, lambda r: r % SEQ * 8 + 2 * k + jnp.where(pair == 0, r // SEQ, 1 - r // SEQ)
        )
        for k in range(TILES)
    ]
    squares = jnp.zeros((2 * ROWS, 1), jnp.float32)
    for j in range(SLOTS):
        f = slots[j]
        comp = jnp.concatenate([rows[s, f, PROMPT_ROWS:, :] for s in range(SEQ)], axis=0)
        comp = [selected(order, comp).astype(jnp.bfloat16) for order in orders]
        comp = jnp.concatenate(comp, axis=1)
        parts = []
        for r in range(2):
            first = 16 * ((pair + r) % 2)
            for s in range(SEQ):
                tiles = [
                    rows[s, f, pl.ds(pl.multiple_of(32 * k + first, 16), 16), :] for k in range(TILES)
                ]
                parts.append(jnp.concatenate(tiles, axis=1))
            parts.append(comp[SEQ * r : SEQ * r + SEQ])
        block = jnp.concatenate(parts, axis=0)
        wide = block.astype(jnp.float32)
        squares = squares + jnp.sum(wide * wide, axis=1, keepdims=True)
        loads[j].wait()
        product = jnp.dot(block, matrix[j], preferred_element_type=jnp.float32)
        if j == 0:
            total[...] = product
        elif j < SLOTS - 1:
            total[...] += product
        else:
            product = total[...] + product
    high = squares.astype(jnp.bfloat16).astype(jnp.float32)
    lane = lax.broadcasted_iota(jnp.int32, (2 * ROWS, HEAD), 1)
    extra = jnp.where(lane == 0, high, jnp.where(lane == 1, squares - high, 0.0))
    width = product.shape[1]
    for r, out in enumerate((own, other)):
        out[:, :width] = product[ROWS * r : ROWS * r + ROWS].astype(jnp.bfloat16)
        out[:, width:] = extra[ROWS * r : ROWS * r + ROWS].astype(jnp.bfloat16)
    sends = [
        pltpu.make_async_copy(other, sent, sem.at[SLOTS]),
        pltpu.make_async_copy(own, kept, sem.at[SLOTS + 1]),
    ]
    for send in sends:
        send.start()
    for send in sends:
        send.wait()


def project(rows, weights):
    depth, width = weights[0].shape
    shape = (ROWS, width + HEAD)
    return pl.pallas_call(
        project_kernel,
        out_shape=(pltpu.HBM(shape, jnp.bfloat16), pltpu.HBM(shape, jnp.bfloat16)),
        in_specs=[whole()] + [whole(pl.ANY)] * SLOTS,
        out_specs=(whole(pltpu.HBM), whole(pltpu.HBM)),
        scratch_shapes=[
            pltpu.VMEM((SLOTS, depth, width), jnp.bfloat16),
            pltpu.VMEM((2 * ROWS, width), jnp.float32),
            pltpu.VMEM(shape, jnp.bfloat16),
            pltpu.VMEM(shape, jnp.bfloat16),
            pltpu.SemaphoreType.DMA((SLOTS + 2,)),
        ],
        compiler_params=pltpu.CompilerParams(vmem_limit_bytes=28 << 20),
        name="project",
    )(rows, *weights)


def rotate_kernel(kept, given, cos_ref, sin_ref, q_ref, kv_ref, held, mine, sem):
    load = pltpu.make_async_copy(kept, mine, sem.at[SAMP])
    load.start()
    load.wait()
    width = (HEADS + 2) * HEAD
    tail = sum(p[:, width:].astype(jnp.float32) for p in (mine, given))
    squares = tail[:, :1] + tail[:, 1:2]
    inv = lax.rsqrt(squares / FEATURES + NORM_EPS)
    cosine, sine = cos_ref[...], sin_ref[...]
    sends = [pltpu.make_async_copy(held, kv_ref.at[m], sem.at[m]) for m in range(SAMP)]
    for h in (HEADS, HEADS + 1, *range(HEADS)):
        columns = pl.ds(h * HEAD, HEAD)
        u = sum(p[:, columns].astype(jnp.float32) for p in (mine, given)) * inv
        if h <= HEADS:
            u = u * cosine + pltpu.roll(u, HEAD // 2, 1) * sine
        if h < HEADS:
            u = u * LOG2_SCALE
        u = u.astype(jnp.bfloat16)
        if h < HEADS:
            q_ref[pl.ds(h * ROWS, ROWS), :] = u
        else:
            held[:, pl.ds((h - HEADS) * HEAD, HEAD)] = u
        if h == HEADS + 1:
            for send in sends:
                send.start()
    for send in sends:
        send.wait()


def rotate(mine, given, cosine, sine):
    return pl.pallas_call(
        rotate_kernel,
        out_shape=(
            jax.ShapeDtypeStruct((HEADS * ROWS, HEAD), jnp.bfloat16),
            pltpu.HBM((SAMP, ROWS, 2 * HEAD), jnp.bfloat16),
        ),
        in_specs=[whole(pl.ANY)] + [whole()] * 3,
        out_specs=(whole(), whole(pltpu.HBM)),
        scratch_shapes=[
            pltpu.VMEM((ROWS, 2 * HEAD), jnp.bfloat16),
            pltpu.VMEM(mine.shape, jnp.bfloat16),
            pltpu.SemaphoreType.DMA((SAMP + 1,)),
        ],
        compiler_params=pltpu.CompilerParams(vmem_limit_bytes=16 << 20),
        name="rotate",
    )(in_hbm(mine), given, cosine, sine)


def prefix_kernel(count, q_ref, kv_ref, acc_out, stat_out, acc_ref, max_ref, sum_ref, sem, *, slots):
    step = pl.program_id(0)

    @pl.when(step == 0)
    def _():
        acc_ref[...] = jnp.zeros_like(acc_ref)
        max_ref[...] = jnp.full_like(max_ref, MASK_FILL)
        sum_ref[...] = jnp.zeros_like(sum_ref)

    first = step * slots

    def absorb(masked):
        keys, values = kv_ref[0, 0], kv_ref[1, 0]
        values = jnp.concatenate([values, jnp.ones_like(values)], axis=1)
        if masked:
            ids = first + lax.broadcasted_iota(jnp.int32, (1, slots), 1)
            bias = jnp.where(ids < count[0], 0.0, MASK_FILL)
        for h in range(HEADS):
            rows = pl.ds(h * ROWS, ROWS)
            scores = lax.dot_general(
                q_ref[rows, :], keys, LAST_DIMS, preferred_element_type=jnp.float32
            )
            if masked:
                scores = scores + bias
            old = max_ref[rows, :]
            new = jnp.maximum(old, jnp.max(scores, axis=1, keepdims=True))
            weights = jnp.exp2(scores - new[:, :1]).astype(jnp.bfloat16)
            factor = jnp.exp2(old - new)
            both = jnp.dot(weights, values, preferred_element_type=jnp.float32)
            acc_ref[rows, :] = acc_ref[rows, :] * factor + both[:, :HEAD]
            sum_ref[rows, :] = sum_ref[rows, :] * factor + both[:, HEAD:]
            max_ref[rows, :] = new

    @pl.when(first + slots <= count[0])
    def _():
        absorb(False)

    @pl.when((first < count[0]) & (first + slots > count[0]))
    def _():
        absorb(True)

    @pl.when(step == pl.num_programs(0) - 1)
    def _():
        lane = lax.broadcasted_iota(jnp.int32, max_ref.shape, 1)
        max_ref[...] = jnp.where(lane < HEAD // 2, max_ref[...], sum_ref[...])
        sends = [
            pltpu.make_async_copy(acc_ref, acc_out, sem.at[0]),
            pltpu.make_async_copy(max_ref, stat_out, sem.at[1]),
        ]
        for send in sends:
            send.start()
        for send in sends:
            send.wait()


def attend_prefix(count, queries, cache, slots=2048):
    n = queries.shape[0]
    state = pltpu.HBM((n, HEAD), jnp.float32)

    def cache_block(step, count):
        return (0, 0, jnp.minimum(step, lax.div(count[0] - 1, slots)), 0)

    return pl.pallas_call(
        functools.partial(prefix_kernel, slots=slots),
        out_shape=(state, state),
        grid_spec=pltpu.PrefetchScalarGridSpec(
            num_scalar_prefetch=1,
            grid=(cache.shape[2] // slots,),
            in_specs=[
                pl.BlockSpec((n, HEAD), lambda step, count: (0, 0)),
                pl.BlockSpec((2, 1, slots, HEAD), cache_block),
            ],
            out_specs=[whole(pltpu.HBM)] * 2,
            scratch_shapes=[pltpu.VMEM((n, HEAD), jnp.float32)] * 3
            + [pltpu.SemaphoreType.DMA((2,))],
        ),
        compiler_params=pltpu.CompilerParams(
            dimension_semantics=("arbitrary",), vmem_limit_bytes=16 << 20
        ),
        name="prefix",
    )(count, queries, cache)


def finish_kernel(q_ref, acc_in, stat_in, kv, out, block, comp_block, acc_ref, stat_ref, sem):
    loads = [
        pltpu.make_async_copy(acc_in, acc_ref, sem.at[GROUPS]),
        pltpu.make_async_copy(stat_in, stat_ref, sem.at[GROUPS + 1]),
    ]
    for load in loads:
        load.start()
    samp_index = lax.axis_index("samp")
    pair, slot = samp_index // 8, samp_index % 8
    keys = jnp.concatenate([kv[m, :PROMPT_ROWS, :HEAD] for m in range(SAMP)], axis=0)
    values = jnp.concatenate([kv[m, :PROMPT_ROWS, HEAD:] for m in range(SAMP)], axis=0)
    values = jnp.concatenate([values, jnp.ones_like(values)], axis=1)
    comp = jnp.concatenate([kv[slot + 8 * r, PROMPT_ROWS:, :] for r in range(2)], axis=0)
    comp_values = jnp.concatenate([comp[:, HEAD:], jnp.ones_like(comp[:, HEAD:])], axis=1)
    n = keys.shape[0]
    column = lax.broadcasted_iota(jnp.int32, (1, n), 1)
    samp = column // PROMPT_ROWS
    key_id = 256 * (column // 16 % SEQ) + 32 * (samp % 8) + 16 * (samp // 8) + column % 16
    row = lax.broadcasted_iota(jnp.int32, (ROWS, 1), 0)
    own_id = 256 * (row // 16) + 32 * slot + 16 * pair + row % 16
    limit = jnp.where(row < PROMPT_ROWS, own_id, n)
    bias = jnp.where(key_id <= limit, 0.0, MASK_FILL)
    column = lax.broadcasted_iota(jnp.int32, (1, 2 * SEQ), 1)
    live = (column % SEQ == row - PROMPT_ROWS) & (column // SEQ <= pair)
    comp_bias = jnp.where(live, 0.0, MASK_FILL)
    for load in loads:
        load.wait()
    for h in range(HEADS):
        rows = pl.ds(h * ROWS, ROWS)
        q = q_ref[rows, :]
        scores = lax.dot_general(q, keys, LAST_DIMS, preferred_element_type=jnp.float32) + bias
        comp_scores = (
            lax.dot_general(q, comp[:, :HEAD], LAST_DIMS, preferred_element_type=jnp.float32)
            + comp_bias
        )
        old, old_sum = stat_ref[rows, :1], stat_ref[rows, HEAD // 2 : HEAD // 2 + 1]
        new = jnp.maximum(old, jnp.max(scores, axis=1, keepdims=True))
        new = jnp.maximum(new, jnp.max(comp_scores, axis=1, keepdims=True))
        weights = jnp.exp2(scores - new[:, :1]).astype(jnp.bfloat16)
        comp_weights = jnp.exp2(comp_scores - new[:, :1]).astype(jnp.bfloat16)
        factor = jnp.exp2(old - new)
        both = jnp.dot(weights, values, preferred_element_type=jnp.float32)
        both = both + jnp.dot(comp_weights, comp_values, preferred_element_type=jnp.float32)
        context = acc_ref[rows, :] * factor + both[:, :HEAD]
        context = context / (old_sum * factor + both[:, HEAD:])
        for s in range(SEQ):
            block[s, pl.ds(16 * h, 16), :] = context[16 * s : 16 * s + 16].astype(jnp.bfloat16)
            comp_block[s, pl.ds(h, 1), :] = context[PROMPT_ROWS + s : PROMPT_ROWS + s + 1]
    for s in range(SEQ):
        block[s, PROMPT_ROWS:, :] = comp_block[s].astype(jnp.bfloat16)

    def send(g):
        return pltpu.make_async_copy(block, out.at[:, g], sem.at[g])

    for g in range(GROUPS):
        send(g).start()
    for g in range(GROUPS):
        send(g).wait()


def finish(queries, state, kv):
    return pl.pallas_call(
        finish_kernel,
        out_shape=pltpu.HBM((SEQ, GROUPS, ROWS, HEAD), jnp.bfloat16),
        in_specs=[whole(), whole(pl.ANY), whole(pl.ANY), whole()],
        out_specs=whole(pltpu.HBM),
        scratch_shapes=[
            pltpu.VMEM((SEQ, ROWS, HEAD), jnp.bfloat16),
            pltpu.VMEM((SEQ, HEADS, HEAD), jnp.float32),
            pltpu.VMEM(queries.shape, jnp.float32),
            pltpu.VMEM(queries.shape, jnp.float32),
            pltpu.SemaphoreType.DMA((GROUPS + 2,)),
        ],
        compiler_params=pltpu.CompilerParams(vmem_limit_bytes=16 << 20),
        name="finish",
    )(queries, *(in_hbm(block) for block in state), kv)


def output_kernel(rest, same, crossed, *refs):
    weights, (prompt_out, comp_out, matrix, sem) = refs[:SEQ], refs[SEQ:]
    loads = [pltpu.make_async_copy(w, matrix.at[j], sem.at[j]) for j, w in enumerate(weights)]
    for load in loads:
        load.start()
    core = lax.axis_index("samp") % 2
    seq = lax.axis_index("seq")
    blocks = (same, crossed)
    n = SAMP * HEADS

    def comp_source(r):
        head, token = r // SAMP, r % SAMP
        group = token % 2 * 4 + token // 4
        crossing = (token // 2 + core) % 2
        return (crossing * GROUPS + group) * HEADS + head

    order = selection(n, n, comp_source)
    total = jnp.zeros((SAMP * 17, matrix.shape[2]), jnp.float32)
    for j in range(SEQ):
        first = moved(seq, SHIFTS[j]) * GROUPS
        left = []
        for b in blocks:
            for g in range(GROUPS):
                parts = [b[first + g, pl.ds(16 * h, 16), :] for h in range(HEADS)]
                left.append(jnp.concatenate(parts, axis=1))
        comp = [b[first + g, PROMPT_ROWS:, :] for b in blocks for g in range(GROUPS)]
        comp = selected(order, jnp.concatenate(comp, axis=0)).astype(jnp.bfloat16)
        parts = [comp[SAMP * h : SAMP * h + SAMP] for h in range(HEADS)]
        left.append(jnp.concatenate(parts, axis=1))
        left = jnp.concatenate(left, axis=0)
        loads[j].wait()
        total = total + jnp.dot(left, matrix[j], preferred_element_type=jnp.float32)
    for r in range(2):
        for g in range(GROUPS):
            slot = 2 * (g % 4) + (core + r) % 2
            at = pl.multiple_of(32 * slot + 16 * (g // 4), 16)
            parts = [
                rest[slot, pl.ds(32 * k + 16 * (g // 4), 16), :].astype(jnp.float32)
                for k in range(TILES)
            ]
            i = 16 * (GROUPS * r + g)
            prompt_out[pl.ds(at, 16), :] = (
                total[i : i + 16] + jnp.concatenate(parts, axis=1)
            ).astype(jnp.bfloat16)
    comp = jnp.concatenate([rest[f, PROMPT_ROWS:, :] for f in range(SLOTS)], axis=0)
    parts = [
        selected(selection(SAMP, 8 * SLOTS, lambda r: r // 2 * 8 + 2 * k + r % 2), comp)
        for k in range(TILES)
    ]
    last = (total[2 * PROMPT_ROWS :] + jnp.concatenate(parts, axis=1)).astype(jnp.bfloat16)
    comp_out[...] = last.reshape(comp_out.shape)


def output(rest, same, crossed, weights):
    width = weights[0].shape[1]
    return pl.pallas_call(
        output_kernel,
        out_shape=(
            jax.ShapeDtypeStruct((2 * PROMPT_ROWS, width), jnp.bfloat16),
            jax.ShapeDtypeStruct((SAMP // 2, 2, width), jnp.bfloat16),
        ),
        in_specs=[whole()] * 3 + [whole(pl.ANY)] * SEQ,
        out_specs=(whole(), whole()),
        scratch_shapes=[
            pltpu.VMEM((SEQ, HEADS * HEAD, width), jnp.bfloat16),
            pltpu.SemaphoreType.DMA((SEQ,)),
        ],
        compiler_params=pltpu.CompilerParams(vmem_limit_bytes=30 << 20),
        name="output",
    )(rest, same, crossed, *weights)


def body(
    prompt_ids,
    comp_ids,
    prefix_len,
    prompt_offset,
    embed_table,
    attn_gain,
    query_key_value_weight,
    w_out,
    key_value_cache,
):
    seq_index = lax.axis_index("seq")
    samp_index = lax.axis_index("samp")
    pair, slot = samp_index // 8, samp_index % 8
    vocab_rows, width = embed_table.shape

    scaled = query_key_value_weight.astype(jnp.float32) * attn_gain.astype(jnp.float32)[:, None]
    scaled = scaled.astype(jnp.bfloat16)
    out_flip = to_seq(w_out, (0, 1))
    w_next, w_last = to_seq(w_out, (3, 0)), to_seq(w_out, (1, 0))
    scaled_next, scaled_last = to_ring(scaled, 3), to_ring(scaled, 1)

    ids = jnp.concatenate([prompt_ids, comp_ids.reshape(-1)])
    local = jnp.clip(ids - seq_index * vocab_rows, 0, vocab_rows - 1)
    picked = embed_table.at[local].get(mode="promise_in_bounds")
    pieces = arrange(picked.reshape(-1, 32, width))
    got = exchange(pieces, ("seq", "samp"), SEQ_SLOT)
    piece_at = SLOTS * seq_index + slot
    own_prompt_ids = lax.dynamic_slice_in_dim(prompt_ids, 32 * piece_at, 32, 0)
    own_comp_ids = lax.dynamic_slice_in_dim(comp_ids.reshape(-1), 2 * piece_at, 2, 0)
    own_ids = jnp.concatenate([jnp.tile(own_prompt_ids, TILES), jnp.tile(own_comp_ids, TILES)])
    owner = (own_ids // vocab_rows)[:, None]
    copies, merged = merge(got, owner)

    rows = exchange(copies, "seq")
    by_ring, _ = lax.optimization_barrier((scaled, copies))
    scaled_far = to_ring(by_ring, 2)
    scales = [scaled, scaled_next, scaled_last, scaled_far]
    scales = scales + [to_other_core(w) for w in scales]
    w_flip, w_last, _ = lax.optimization_barrier((out_flip, w_last, scaled_far))
    w_next_flip, w_last_flip = to_seq(w_flip, (3, 0)), to_seq(w_flip, (1, 0))
    w_far = to_seq(w_last, (1, 0))

    mine, sent = project(rows, scales)
    given = to_other_pair(sent)
    rest = exchange(merged, "samp", SAME_PAIR)
    given, rest = lax.optimization_barrier((given, rest))

    row = jnp.arange(ROWS, dtype=jnp.int32)
    own_prompt = 256 * (row // 16) + 32 * slot + 16 * pair + row % 16
    position = jnp.where(row < PROMPT_ROWS, own_prompt, 2048 + pair) + prompt_offset[0]
    angles = position.astype(jnp.float32)[:, None] * rope_freqs(HEAD)[None, :]
    cosine, sine = jnp.cos(angles), jnp.sin(angles)
    cosine = jnp.concatenate([cosine, cosine], axis=1)
    sine = jnp.concatenate([-sine, sine], axis=1)
    queries, kv = rotate(mine, given, cosine, sine)
    all_kv = exchange(kv, "samp")
    queries, w_next_flip = lax.optimization_barrier((queries, w_next_flip))
    w_far_flip = to_seq(w_next_flip, (3, 0))
    state = attend_prefix(
        prefix_len, queries, pltpu.with_memory_space_constraint(key_value_cache, pltpu.HBM)
    )
    weights = [w_out, w_flip, w_next, w_next_flip, w_last, w_last_flip, w_far, w_far_flip]
    context = finish(queries, state, all_kv)
    context = context.reshape(SEQ * GROUPS, ROWS, HEAD)

    same = exchange(context, ("seq", "samp"), SEQ_GROUP)
    crossed = to_other_core(same)
    prompt_out, comp_out = output(rest, same, crossed, weights)
    return prompt_out, comp_out


def solution(mesh):
    placed = (
        P(),
        P(),
        P(),
        P(),
        P("seq", "samp"),
        P("samp"),
        P("samp", "seq"),
        P("seq", "samp"),
        P(None, "seq", None, None),
    )
    return jax.shard_map(
        body,
        mesh=mesh,
        in_specs=placed,
        out_specs=(P("seq", "samp"), P("seq", None, "samp")),
        check_vma=False,
    )
```

```python
import functools
import math

import jax
import jax.numpy as jnp
from jax import lax
from jax.experimental import pallas as pl
from jax.experimental.pallas import tpu as pltpu
from jax.sharding import PartitionSpec as P


NORM_EPS = 1e-05
MASK_FILL = -1e30
HEAD = 128
HEADS = 8
SEQ = 8
GROUPS = 8
SAMP = 16
ROWS = 136
PROMPT_ROWS = 128
FEATURES = 8192
LOG2_SCALE = math.log2(math.e) / math.sqrt(HEAD)
LAST_DIMS = (((1,), (1,)), ((), ()))

SLOTS = 8
TILES = 4
SEQ_SLOT = [[SAMP * s + 8 * pair + f for s in range(SEQ) for f in range(SLOTS)] for pair in range(2)]
SAME_PAIR = [[8 * pair + f for f in range(SLOTS)] for pair in range(2)]
SEQ_GROUP = [[SAMP * s + 2 * g + c for s in range(SEQ) for g in range(GROUPS)] for c in range(2)]
SHIFTS = ((0, 0), (0, 1), (1, 0), (1, 1), (3, 0), (3, 1), (2, 0), (2, 1))


def rope_freqs(head_dim):
    half_dim = head_dim // 2
    dim_index = jnp.arange(half_dim, dtype=jnp.float32)
    base_freq = 1.0 / jnp.power(500000.0, 2.0 * dim_index / head_dim)
    wavelength = 2.0 * math.pi / base_freq
    blend = (8192.0 / wavelength - 1.0) / 3.0
    middle = (1.0 - blend) * base_freq / 8.0 + blend * base_freq
    return jnp.where(
        wavelength > 8192.0, base_freq / 8.0, jnp.where(wavelength < 2048.0, base_freq, middle)
    )


def moved(index, shift, sign=1):
    return (index % 4 + sign * shift[0] + 4) % 4 + 4 * ((index // 4) ^ shift[1])


def to_seq(block, shift):
    return lax.ppermute(block, "seq", [(i, moved(i, shift)) for i in range(SEQ)])


def to_other_core(block):
    return lax.ppermute(block, "samp", [(i, i ^ 1) for i in range(SAMP)])


def to_ring(block, step):
    pairs = [(m, m // 8 * 8 + (m % 8 + 2 * step) % 8) for m in range(SAMP)]
    return lax.ppermute(block, "samp", pairs)


def to_other_pair(block):
    return lax.ppermute(block, "samp", [(m, (m + 8) % SAMP) for m in range(SAMP)])


def exchange(blocks, axes, groups=None):
    return lax.all_to_all(blocks, axes, 0, 0, tiled=True, axis_index_groups=groups)


def whole(memory_space=pltpu.VMEM):
    return pl.BlockSpec(memory_space=memory_space)


def in_hbm(block):
    return pltpu.with_memory_space_constraint(block, pltpu.HBM)


def selection(rows, columns, wanted):
    row = lax.broadcasted_iota(jnp.int32, (rows, columns), 0)
    column = lax.broadcasted_iota(jnp.int32, (rows, columns), 1)
    return jnp.where(column == wanted(row), 1.0, 0.0).astype(jnp.bfloat16)


def selected(matrix, block):
    return jnp.dot(matrix, block, preferred_element_type=jnp.float32)


def arrange_kernel(picked, out, comp, sem):
    n = SEQ * SLOTS
    sends = [
        pltpu.make_async_copy(
            picked.at[pl.ds(0, n), :, pl.ds(HEAD * k, HEAD)], out.at[:, pl.ds(32 * k, 32), :], sem.at[k]
        )
        for k in range(TILES)
    ]
    for send in sends:
        send.start()
    rows = jnp.concatenate([picked[n + i] for i in range(4)], axis=0)
    total = jnp.zeros((8 * n, HEAD), jnp.float32)
    for k in range(TILES):
        matrix = selection(
            8 * n, 2 * n, lambda r: jnp.where(r // 2 % TILES == k, r // 8 * 2 + r % 2, -1)
        )
        total = total + selected(matrix, rows[:, HEAD * k : HEAD * k + HEAD])
    comp[...] = total.astype(jnp.bfloat16).reshape(n, 8, HEAD)
    last = pltpu.make_async_copy(comp, out.at[:, pl.ds(PROMPT_ROWS, 8), :], sem.at[TILES])
    last.start()
    for send in sends + [last]:
        send.wait()


def arrange(picked):
    n = SEQ * SLOTS
    return pl.pallas_call(
        arrange_kernel,
        out_shape=pltpu.HBM((n, ROWS, HEAD), jnp.bfloat16),
        in_specs=[whole()],
        out_specs=whole(pltpu.HBM),
        scratch_shapes=[
            pltpu.VMEM((n, 8, HEAD), jnp.bfloat16),
            pltpu.SemaphoreType.DMA((TILES + 1,)),
        ],
        compiler_params=pltpu.CompilerParams(vmem_limit_bytes=16 << 20),
        name="arrange",
    )(picked)


def merge_kernel(got, owners, copies, merged, held, owner, sem):
    load = pltpu.make_async_copy(owners, owner, sem.at[SEQ + 1])
    load.start()
    load.wait()
    sends = [pltpu.make_async_copy(held, copies.at[s], sem.at[s]) for s in range(SEQ)]
    sends.append(pltpu.make_async_copy(held, merged, sem.at[SEQ]))
    owns = [owner[...] == s for s in range(SEQ)]
    for f in range(SLOTS):
        total = jnp.zeros((ROWS, HEAD), jnp.float32)
        for s in range(SEQ):
            total = jnp.where(owns[s], got[SLOTS * s + f].astype(jnp.float32), total)
        held[f] = total.astype(jnp.bfloat16)
    for send in sends:
        send.start()
    for send in sends:
        send.wait()


def merge(got, owner):
    return pl.pallas_call(
        merge_kernel,
        out_shape=(
            pltpu.HBM((SEQ, SLOTS, ROWS, HEAD), jnp.bfloat16),
            pltpu.HBM((SLOTS, ROWS, HEAD), jnp.bfloat16),
        ),
        in_specs=[whole(), whole(pl.ANY)],
        out_specs=(whole(pltpu.HBM), whole(pltpu.HBM)),
        scratch_shapes=[
            pltpu.VMEM((SLOTS, ROWS, HEAD), jnp.bfloat16),
            pltpu.VMEM((ROWS, 1), jnp.int32),
            pltpu.SemaphoreType.DMA((SEQ + 2,)),
        ],
        compiler_params=pltpu.CompilerParams(vmem_limit_bytes=16 << 20),
        name="merge",
    )(got, in_hbm(owner))


def project_kernel(rows, *refs):
    weights, (kept, sent, matrix, total, own, other, sem) = refs[:SLOTS], refs[SLOTS:]
    loads = [pltpu.make_async_copy(w, matrix.at[j], sem.at[j]) for j, w in enumerate(weights)]
    for load in loads:
        load.start()
    samp = lax.axis_index("samp")
    pair, slot = samp // 8, samp % 8
    slots = [(slot // 2 + step) % 4 * 2 + (slot + cross) % 2 for cross in (0, 1) for step in (0, 1, 3, 2)]
    n = 8 * SEQ
    orders = [
        selection(
            2 * SEQ, n, lambda r: r % SEQ * 8 + 2 * k + jnp.where(pair == 0, r // SEQ, 1 - r // SEQ)
        )
        for k in range(TILES)
    ]
    squares = jnp.zeros((2 * ROWS, 1), jnp.float32)
    for j in range(SLOTS):
        f = slots[j]
        comp = jnp.concatenate([rows[s, f, PROMPT_ROWS:, :] for s in range(SEQ)], axis=0)
        comp = [selected(order, comp).astype(jnp.bfloat16) for order in orders]
        comp = jnp.concatenate(comp, axis=1)
        parts = []
        for r in range(2):
            first = 16 * ((pair + r) % 2)
            for s in range(SEQ):
                tiles = [
                    rows[s, f, pl.ds(pl.multiple_of(32 * k + first, 16), 16), :] for k in range(TILES)
                ]
                parts.append(jnp.concatenate(tiles, axis=1))
            parts.append(comp[SEQ * r : SEQ * r + SEQ])
        block = jnp.concatenate(parts, axis=0)
        wide = block.astype(jnp.float32)
        squares = squares + jnp.sum(wide * wide, axis=1, keepdims=True)
        loads[j].wait()
        product = jnp.dot(block, matrix[j], preferred_element_type=jnp.float32)
        if j == 0:
            total[...] = product
        elif j < SLOTS - 1:
            total[...] += product
        else:
            product = total[...] + product
    high = squares.astype(jnp.bfloat16).astype(jnp.float32)
    lane = lax.broadcasted_iota(jnp.int32, (2 * ROWS, HEAD), 1)
    extra = jnp.where(lane == 0, high, jnp.where(lane == 1, squares - high, 0.0))
    width = product.shape[1]
    for r, out in enumerate((own, other)):
        out[:, :width] = product[ROWS * r : ROWS * r + ROWS].astype(jnp.bfloat16)
        out[:, width:] = extra[ROWS * r : ROWS * r + ROWS].astype(jnp.bfloat16)
    sends = [
        pltpu.make_async_copy(other, sent, sem.at[SLOTS]),
        pltpu.make_async_copy(own, kept, sem.at[SLOTS + 1]),
    ]
    for send in sends:
        send.start()
    for send in sends:
        send.wait()


def project(rows, weights):
    depth, width = weights[0].shape
    shape = (ROWS, width + HEAD)
    return pl.pallas_call(
        project_kernel,
        out_shape=(pltpu.HBM(shape, jnp.bfloat16), pltpu.HBM(shape, jnp.bfloat16)),
        in_specs=[whole()] + [whole(pl.ANY)] * SLOTS,
        out_specs=(whole(pltpu.HBM), whole(pltpu.HBM)),
        scratch_shapes=[
            pltpu.VMEM((SLOTS, depth, width), jnp.bfloat16),
            pltpu.VMEM((2 * ROWS, width), jnp.float32),
            pltpu.VMEM(shape, jnp.bfloat16),
            pltpu.VMEM(shape, jnp.bfloat16),
            pltpu.SemaphoreType.DMA((SLOTS + 2,)),
        ],
        compiler_params=pltpu.CompilerParams(vmem_limit_bytes=28 << 20),
        name="project",
    )(rows, *weights)


def rotate_kernel(kept, given, cos_ref, sin_ref, q_ref, kv_ref, held, mine, sem):
    load = pltpu.make_async_copy(kept, mine, sem.at[SAMP])
    load.start()
    load.wait()
    width = (HEADS + 2) * HEAD
    tail = sum(p[:, width:].astype(jnp.float32) for p in (mine, given))
    squares = tail[:, :1] + tail[:, 1:2]
    inv = lax.rsqrt(squares / FEATURES + NORM_EPS)
    cosine, sine = cos_ref[...], sin_ref[...]
    sends = [pltpu.make_async_copy(held, kv_ref.at[m], sem.at[m]) for m in range(SAMP)]
    for h in (HEADS, HEADS + 1, *range(HEADS)):
        columns = pl.ds(h * HEAD, HEAD)
        u = sum(p[:, columns].astype(jnp.float32) for p in (mine, given)) * inv
        if h <= HEADS:
            u = u * cosine + pltpu.roll(u, HEAD // 2, 1) * sine
        if h < HEADS:
            u = u * LOG2_SCALE
        u = u.astype(jnp.bfloat16)
        if h < HEADS:
            q_ref[pl.ds(h * ROWS, ROWS), :] = u
        else:
            held[:, pl.ds((h - HEADS) * HEAD, HEAD)] = u
        if h == HEADS + 1:
            for send in sends:
                send.start()
    for send in sends:
        send.wait()


def rotate(mine, given, cosine, sine):
    return pl.pallas_call(
        rotate_kernel,
        out_shape=(
            jax.ShapeDtypeStruct((HEADS * ROWS, HEAD), jnp.bfloat16),
            pltpu.HBM((SAMP, ROWS, 2 * HEAD), jnp.bfloat16),
        ),
        in_specs=[whole(pl.ANY)] + [whole()] * 3,
        out_specs=(whole(), whole(pltpu.HBM)),
        scratch_shapes=[
            pltpu.VMEM((ROWS, 2 * HEAD), jnp.bfloat16),
            pltpu.VMEM(mine.shape, jnp.bfloat16),
            pltpu.SemaphoreType.DMA((SAMP + 1,)),
        ],
        compiler_params=pltpu.CompilerParams(vmem_limit_bytes=16 << 20),
        name="rotate",
    )(in_hbm(mine), given, cosine, sine)


def prefix_kernel(count, q_ref, kv_ref, acc_out, stat_out, acc_ref, max_ref, sum_ref, sem, *, slots):
    step = pl.program_id(0)

    @pl.when(step == 0)
    def _():
        acc_ref[...] = jnp.zeros_like(acc_ref)
        max_ref[...] = jnp.full_like(max_ref, MASK_FILL)
        sum_ref[...] = jnp.zeros_like(sum_ref)

    first = step * slots

    def absorb(masked):
        keys, values = kv_ref[0, 0], kv_ref[1, 0]
        values = jnp.concatenate([values, jnp.ones_like(values)], axis=1)
        if masked:
            ids = first + lax.broadcasted_iota(jnp.int32, (1, slots), 1)
            bias = jnp.where(ids < count[0], 0.0, MASK_FILL)
        for h in range(HEADS):
            rows = pl.ds(h * ROWS, ROWS)
            scores = lax.dot_general(
                q_ref[rows, :], keys, LAST_DIMS, preferred_element_type=jnp.float32
            )
            if masked:
                scores = scores + bias
            old = max_ref[rows, :]
            new = jnp.maximum(old, jnp.max(scores, axis=1, keepdims=True))
            weights = jnp.exp2(scores - new[:, :1]).astype(jnp.bfloat16)
            factor = jnp.exp2(old - new)
            both = jnp.dot(weights, values, preferred_element_type=jnp.float32)
            acc_ref[rows, :] = acc_ref[rows, :] * factor + both[:, :HEAD]
            sum_ref[rows, :] = sum_ref[rows, :] * factor + both[:, HEAD:]
            max_ref[rows, :] = new

    @pl.when(first + slots <= count[0])
    def _():
        absorb(False)

    @pl.when((first < count[0]) & (first + slots > count[0]))
    def _():
        absorb(True)

    @pl.when(step == pl.num_programs(0) - 1)
    def _():
        lane = lax.broadcasted_iota(jnp.int32, max_ref.shape, 1)
        max_ref[...] = jnp.where(lane < HEAD // 2, max_ref[...], sum_ref[...])
        sends = [
            pltpu.make_async_copy(acc_ref, acc_out, sem.at[0]),
            pltpu.make_async_copy(max_ref, stat_out, sem.at[1]),
        ]
        for send in sends:
            send.start()
        for send in sends:
            send.wait()


def attend_prefix(count, queries, cache, slots=2048):
    n = queries.shape[0]
    state = pltpu.HBM((n, HEAD), jnp.float32)

    def cache_block(step, count):
        return (0, 0, jnp.minimum(step, lax.div(count[0] - 1, slots)), 0)

    return pl.pallas_call(
        functools.partial(prefix_kernel, slots=slots),
        out_shape=(state, state),
        grid_spec=pltpu.PrefetchScalarGridSpec(
            num_scalar_prefetch=1,
            grid=(cache.shape[2] // slots,),
            in_specs=[
                pl.BlockSpec((n, HEAD), lambda step, count: (0, 0)),
                pl.BlockSpec((2, 1, slots, HEAD), cache_block),
            ],
            out_specs=[whole(pltpu.HBM)] * 2,
            scratch_shapes=[pltpu.VMEM((n, HEAD), jnp.float32)] * 3
            + [pltpu.SemaphoreType.DMA((2,))],
        ),
        compiler_params=pltpu.CompilerParams(
            dimension_semantics=("arbitrary",), vmem_limit_bytes=16 << 20
        ),
        name="prefix",
    )(count, queries, cache)


def finish_kernel(q_ref, acc_in, stat_in, kv, out, block, comp_block, acc_ref, stat_ref, sem):
    loads = [
        pltpu.make_async_copy(acc_in, acc_ref, sem.at[GROUPS]),
        pltpu.make_async_copy(stat_in, stat_ref, sem.at[GROUPS + 1]),
    ]
    for load in loads:
        load.start()
    samp_index = lax.axis_index("samp")
    pair, slot = samp_index // 8, samp_index % 8
    keys = jnp.concatenate([kv[m, :PROMPT_ROWS, :HEAD] for m in range(SAMP)], axis=0)
    values = jnp.concatenate([kv[m, :PROMPT_ROWS, HEAD:] for m in range(SAMP)], axis=0)
    values = jnp.concatenate([values, jnp.ones_like(values)], axis=1)
    comp = jnp.concatenate([kv[slot + 8 * r, PROMPT_ROWS:, :] for r in range(2)], axis=0)
    comp_values = jnp.concatenate([comp[:, HEAD:], jnp.ones_like(comp[:, HEAD:])], axis=1)
    n = keys.shape[0]
    column = lax.broadcasted_iota(jnp.int32, (1, n), 1)
    samp = column // PROMPT_ROWS
    key_id = 256 * (column // 16 % SEQ) + 32 * (samp % 8) + 16 * (samp // 8) + column % 16
    row = lax.broadcasted_iota(jnp.int32, (ROWS, 1), 0)
    own_id = 256 * (row // 16) + 32 * slot + 16 * pair + row % 16
    limit = jnp.where(row < PROMPT_ROWS, own_id, n)
    bias = jnp.where(key_id <= limit, 0.0, MASK_FILL)
    column = lax.broadcasted_iota(jnp.int32, (1, 2 * SEQ), 1)
    live = (column % SEQ == row - PROMPT_ROWS) & (column // SEQ <= pair)
    comp_bias = jnp.where(live, 0.0, MASK_FILL)
    for load in loads:
        load.wait()
    for h in range(HEADS):
        rows = pl.ds(h * ROWS, ROWS)
        q = q_ref[rows, :]
        scores = lax.dot_general(q, keys, LAST_DIMS, preferred_element_type=jnp.float32) + bias
        comp_scores = (
            lax.dot_general(q, comp[:, :HEAD], LAST_DIMS, preferred_element_type=jnp.float32)
            + comp_bias
        )
        old, old_sum = stat_ref[rows, :1], stat_ref[rows, HEAD // 2 : HEAD // 2 + 1]
        new = jnp.maximum(old, jnp.max(scores, axis=1, keepdims=True))
        new = jnp.maximum(new, jnp.max(comp_scores, axis=1, keepdims=True))
        weights = jnp.exp2(scores - new[:, :1]).astype(jnp.bfloat16)
        comp_weights = jnp.exp2(comp_scores - new[:, :1]).astype(jnp.bfloat16)
        factor = jnp.exp2(old - new)
        both = jnp.dot(weights, values, preferred_element_type=jnp.float32)
        both = both + jnp.dot(comp_weights, comp_values, preferred_element_type=jnp.float32)
        context = acc_ref[rows, :] * factor + both[:, :HEAD]
        context = context / (old_sum * factor + both[:, HEAD:])
        for s in range(SEQ):
            block[s, pl.ds(16 * h, 16), :] = context[16 * s : 16 * s + 16].astype(jnp.bfloat16)
            comp_block[s, pl.ds(h, 1), :] = context[PROMPT_ROWS + s : PROMPT_ROWS + s + 1]
    for s in range(SEQ):
        block[s, PROMPT_ROWS:, :] = comp_block[s].astype(jnp.bfloat16)

    def send(g):
        return pltpu.make_async_copy(block, out.at[:, g], sem.at[g])

    for g in range(GROUPS):
        send(g).start()
    for g in range(GROUPS):
        send(g).wait()


def finish(queries, state, kv):
    return pl.pallas_call(
        finish_kernel,
        out_shape=pltpu.HBM((SEQ, GROUPS, ROWS, HEAD), jnp.bfloat16),
        in_specs=[whole(), whole(pl.ANY), whole(pl.ANY), whole()],
        out_specs=whole(pltpu.HBM),
        scratch_shapes=[
            pltpu.VMEM((SEQ, ROWS, HEAD), jnp.bfloat16),
            pltpu.VMEM((SEQ, HEADS, HEAD), jnp.float32),
            pltpu.VMEM(queries.shape, jnp.float32),
            pltpu.VMEM(queries.shape, jnp.float32),
            pltpu.SemaphoreType.DMA((GROUPS + 2,)),
        ],
        compiler_params=pltpu.CompilerParams(vmem_limit_bytes=16 << 20),
        name="finish",
    )(queries, *(in_hbm(block) for block in state), kv)


def products(block, matrix, ready):
    n = GROUPS * HEADS
    order = selection(n, n, lambda r: r % GROUPS * HEADS + r // GROUPS)
    seq = lax.axis_index("seq")
    total = jnp.zeros((ROWS, matrix.shape[2]), jnp.float32)
    for j in range(SEQ):
        first = moved(seq, SHIFTS[j]) * GROUPS
        left = []
        for g in range(GROUPS):
            parts = [block[first + g, pl.ds(16 * h, 16), :] for h in range(HEADS)]
            left.append(jnp.concatenate(parts, axis=1))
        comp = jnp.concatenate([block[first + g, PROMPT_ROWS:, :] for g in range(GROUPS)], axis=0)
        comp = selected(order, comp)
        parts = [comp[GROUPS * h : GROUPS * h + GROUPS] for h in range(HEADS)]
        left.append(jnp.concatenate(parts, axis=1).astype(jnp.bfloat16))
        left = jnp.concatenate(left, axis=0)
        ready(j)
        total = total + jnp.dot(left, matrix[j], preferred_element_type=jnp.float32)
    return total


def near_kernel(same, *refs):
    weights, (total, matrix, sem) = refs[:SEQ], refs[SEQ:]
    loads = [pltpu.make_async_copy(w, matrix.at[j], sem.at[j]) for j, w in enumerate(weights)]
    for load in loads:
        load.start()
    total[...] = products(same, matrix, lambda j: loads[j].wait())


def near_output(same, weights):
    depth, width = weights[0].shape
    return pl.pallas_call(
        near_kernel,
        out_shape=(
            jax.ShapeDtypeStruct((ROWS, width), jnp.float32),
            pltpu.VMEM((SEQ, depth, width), jnp.bfloat16),
        ),
        in_specs=[whole()] + [whole(pl.ANY)] * SEQ,
        out_specs=(whole(), whole()),
        scratch_shapes=[pltpu.SemaphoreType.DMA((SEQ,))],
        compiler_params=pltpu.CompilerParams(vmem_limit_bytes=18 << 20),
        name="near_output",
    )(same, *weights)


def far_kernel(rest, crossed, near, matrix, prompt_out, comp_out):
    core = lax.axis_index("samp") % 2
    totals = (near[...], products(crossed, matrix, lambda j: None))
    for r in range(2):
        for g in range(GROUPS):
            slot = 2 * (g % 4) + (core + r) % 2
            at = pl.multiple_of(32 * slot + 16 * (g // 4), 16)
            parts = [
                rest[slot, pl.ds(32 * k + 16 * (g // 4), 16), :].astype(jnp.float32)
                for k in range(TILES)
            ]
            prompt_out[pl.ds(at, 16), :] = (
                totals[r][16 * g : 16 * g + 16] + jnp.concatenate(parts, axis=1)
            ).astype(jnp.bfloat16)
    comp = jnp.concatenate([rest[f, PROMPT_ROWS:, :] for f in range(SLOTS)], axis=0)

    def rest_of(r, k):
        slot = 2 * (r % 4) + (r // GROUPS + core) % 2
        return slot * 8 + 2 * k + r % GROUPS // 4

    parts = [
        selected(selection(SAMP, 8 * SLOTS, lambda r: rest_of(r, k)), comp) for k in range(TILES)
    ]
    last = jnp.concatenate([t[PROMPT_ROWS:] for t in totals], axis=0)
    last = (last + jnp.concatenate(parts, axis=1)).astype(jnp.bfloat16)
    order = selection(
        SAMP, SAMP, lambda r: (r // 2 + core) % 2 * GROUPS + r % 2 * 4 + r // 4
    )
    comp_out[...] = selected(order, last).astype(jnp.bfloat16).reshape(comp_out.shape)


def far_output(rest, crossed, near, matrix):
    width = near.shape[1]
    return pl.pallas_call(
        far_kernel,
        out_shape=(
            jax.ShapeDtypeStruct((2 * PROMPT_ROWS, width), jnp.bfloat16),
            jax.ShapeDtypeStruct((SAMP // 2, 2, width), jnp.bfloat16),
        ),
        in_specs=[whole()] * 4,
        out_specs=(whole(), whole()),
        compiler_params=pltpu.CompilerParams(vmem_limit_bytes=22 << 20),
        name="far_output",
    )(rest, crossed, near, matrix)


def body(
    prompt_ids,
    comp_ids,
    prefix_len,
    prompt_offset,
    embed_table,
    attn_gain,
    query_key_value_weight,
    w_out,
    key_value_cache,
):
    seq_index = lax.axis_index("seq")
    samp_index = lax.axis_index("samp")
    pair, slot = samp_index // 8, samp_index % 8
    vocab_rows, width = embed_table.shape

    scaled = query_key_value_weight.astype(jnp.float32) * attn_gain.astype(jnp.float32)[:, None]
    scaled = scaled.astype(jnp.bfloat16)
    out_flip = to_seq(w_out, (0, 1))
    w_next, w_last = to_seq(w_out, (3, 0)), to_seq(w_out, (1, 0))
    scaled_next, scaled_last = to_ring(scaled, 3), to_ring(scaled, 1)

    ids = jnp.concatenate([prompt_ids, comp_ids.reshape(-1)])
    local = jnp.clip(ids - seq_index * vocab_rows, 0, vocab_rows - 1)
    picked = embed_table.at[local].get(mode="promise_in_bounds")
    pieces = arrange(picked.reshape(-1, 32, width))
    got = exchange(pieces, ("seq", "samp"), SEQ_SLOT)
    piece_at = SLOTS * seq_index + slot
    own_prompt_ids = lax.dynamic_slice_in_dim(prompt_ids, 32 * piece_at, 32, 0)
    own_comp_ids = lax.dynamic_slice_in_dim(comp_ids.reshape(-1), 2 * piece_at, 2, 0)
    own_ids = jnp.concatenate([jnp.tile(own_prompt_ids, TILES), jnp.tile(own_comp_ids, TILES)])
    owner = (own_ids // vocab_rows)[:, None]
    copies, merged = merge(got, owner)

    rows = exchange(copies, "seq")
    by_ring, _ = lax.optimization_barrier((scaled, copies))
    scaled_far = to_ring(by_ring, 2)
    scales = [scaled, scaled_next, scaled_last, scaled_far]
    scales = scales + [to_other_core(w) for w in scales]
    w_flip, w_last, _ = lax.optimization_barrier((out_flip, w_last, scaled_far))
    w_next_flip, w_last_flip = to_seq(w_flip, (3, 0)), to_seq(w_flip, (1, 0))
    w_far = to_seq(w_last, (1, 0))

    mine, sent = project(rows, scales)
    given = to_other_pair(sent)
    rest = exchange(merged, "samp", SAME_PAIR)
    given, rest = lax.optimization_barrier((given, rest))

    row = jnp.arange(ROWS, dtype=jnp.int32)
    own_prompt = 256 * (row // 16) + 32 * slot + 16 * pair + row % 16
    position = jnp.where(row < PROMPT_ROWS, own_prompt, 2048 + pair) + prompt_offset[0]
    angles = position.astype(jnp.float32)[:, None] * rope_freqs(HEAD)[None, :]
    cosine, sine = jnp.cos(angles), jnp.sin(angles)
    cosine = jnp.concatenate([cosine, cosine], axis=1)
    sine = jnp.concatenate([-sine, sine], axis=1)
    queries, kv = rotate(mine, given, cosine, sine)
    all_kv = exchange(kv, "samp")
    queries, w_next_flip = lax.optimization_barrier((queries, w_next_flip))
    w_far_flip = to_seq(w_next_flip, (3, 0))
    state = attend_prefix(
        prefix_len, queries, pltpu.with_memory_space_constraint(key_value_cache, pltpu.HBM)
    )
    weights = [w_out, w_flip, w_next, w_next_flip, w_last, w_last_flip, w_far, w_far_flip]
    context = finish(queries, state, all_kv)
    context = context.reshape(SEQ * GROUPS, ROWS, HEAD)

    same = exchange(context, ("seq", "samp"), SEQ_GROUP)
    crossed = to_other_core(same)
    near, matrix = near_output(same, weights)
    prompt_out, comp_out = far_output(rest, crossed, near, matrix)
    return prompt_out, comp_out


def solution(mesh):
    placed = (
        P(),
        P(),
        P(),
        P(),
        P("seq", "samp"),
        P("samp"),
        P("samp", "seq"),
        P("seq", "samp"),
        P(None, "seq", None, None),
    )
    return jax.shard_map(
        body,
        mesh=mesh,
        in_specs=placed,
        out_specs=(P("seq", "samp"), P("seq", None, "samp")),
        check_vma=False,
    )
```

```python
import functools
import math

import jax
import jax.numpy as jnp
from jax import lax
from jax.experimental import pallas as pl
from jax.experimental.pallas import tpu as pltpu
from jax.sharding import PartitionSpec as P


NORM_EPS = 1e-05
MASK_FILL = -1e30
HEAD = 128
HEADS = 8
SEQ = 8
GROUPS = 8
SAMP = 16
ROWS = 136
PROMPT_ROWS = 128
FEATURES = 8192
LOG2_SCALE = math.log2(math.e) / math.sqrt(HEAD)
LAST_DIMS = (((1,), (1,)), ((), ()))

SLOTS = 8
TILES = 4
SEQ_SLOT = [[SAMP * s + 8 * pair + f for s in range(SEQ) for f in range(SLOTS)] for pair in range(2)]
SAME_PAIR = [[8 * pair + f for f in range(SLOTS)] for pair in range(2)]
SEQ_GROUP = [[SAMP * s + 2 * g + c for s in range(SEQ) for g in range(GROUPS)] for c in range(2)]
SHIFTS = ((0, 0), (0, 1), (1, 0), (1, 1), (3, 0), (3, 1), (2, 0), (2, 1))


def rope_freqs(head_dim):
    half_dim = head_dim // 2
    dim_index = jnp.arange(half_dim, dtype=jnp.float32)
    base_freq = 1.0 / jnp.power(500000.0, 2.0 * dim_index / head_dim)
    wavelength = 2.0 * math.pi / base_freq
    blend = (8192.0 / wavelength - 1.0) / 3.0
    middle = (1.0 - blend) * base_freq / 8.0 + blend * base_freq
    return jnp.where(
        wavelength > 8192.0, base_freq / 8.0, jnp.where(wavelength < 2048.0, base_freq, middle)
    )


def moved(index, shift, sign=1):
    return (index % 4 + sign * shift[0] + 4) % 4 + 4 * ((index // 4) ^ shift[1])


def to_seq(block, shift):
    return lax.ppermute(block, "seq", [(i, moved(i, shift)) for i in range(SEQ)])


def to_other_core(block):
    return lax.ppermute(block, "samp", [(i, i ^ 1) for i in range(SAMP)])


def to_ring(block, step):
    pairs = [(m, m // 8 * 8 + (m % 8 + 2 * step) % 8) for m in range(SAMP)]
    return lax.ppermute(block, "samp", pairs)


def to_other_pair(block):
    return lax.ppermute(block, "samp", [(m, (m + 8) % SAMP) for m in range(SAMP)])


def exchange(blocks, axes, groups=None):
    return lax.all_to_all(blocks, axes, 0, 0, tiled=True, axis_index_groups=groups)


def whole(memory_space=pltpu.VMEM):
    return pl.BlockSpec(memory_space=memory_space)


def in_hbm(block):
    return pltpu.with_memory_space_constraint(block, pltpu.HBM)


def selection(rows, columns, wanted):
    row = lax.broadcasted_iota(jnp.int32, (rows, columns), 0)
    column = lax.broadcasted_iota(jnp.int32, (rows, columns), 1)
    return jnp.where(column == wanted(row), 1.0, 0.0).astype(jnp.bfloat16)


def selected(matrix, block):
    return jnp.dot(matrix, block, preferred_element_type=jnp.float32)


def arrange_kernel(picked, out, comp, sem):
    n = SEQ * SLOTS
    sends = [
        pltpu.make_async_copy(
            picked.at[pl.ds(0, n), :, pl.ds(HEAD * k, HEAD)], out.at[:, pl.ds(32 * k, 32), :], sem.at[k]
        )
        for k in range(TILES)
    ]
    for send in sends:
        send.start()
    rows = jnp.concatenate([picked[n + i] for i in range(4)], axis=0)
    total = jnp.zeros((8 * n, HEAD), jnp.float32)
    for k in range(TILES):
        matrix = selection(
            8 * n, 2 * n, lambda r: jnp.where(r // 2 % TILES == k, r // 8 * 2 + r % 2, -1)
        )
        total = total + selected(matrix, rows[:, HEAD * k : HEAD * k + HEAD])
    comp[...] = total.astype(jnp.bfloat16).reshape(n, 8, HEAD)
    last = pltpu.make_async_copy(comp, out.at[:, pl.ds(PROMPT_ROWS, 8), :], sem.at[TILES])
    last.start()
    for send in sends + [last]:
        send.wait()


def arrange(picked):
    n = SEQ * SLOTS
    return pl.pallas_call(
        arrange_kernel,
        out_shape=pltpu.HBM((n, ROWS, HEAD), jnp.bfloat16),
        in_specs=[whole()],
        out_specs=whole(pltpu.HBM),
        scratch_shapes=[
            pltpu.VMEM((n, 8, HEAD), jnp.bfloat16),
            pltpu.SemaphoreType.DMA((TILES + 1,)),
        ],
        compiler_params=pltpu.CompilerParams(vmem_limit_bytes=16 << 20),
        name="arrange",
    )(picked)


def merge_kernel(got, owners, copies, merged, held, owner, sem):
    load = pltpu.make_async_copy(owners, owner, sem.at[SEQ + 1])
    load.start()
    load.wait()
    sends = [pltpu.make_async_copy(held, copies.at[s], sem.at[s]) for s in range(SEQ)]
    sends.append(pltpu.make_async_copy(held, merged, sem.at[SEQ]))
    owns = [owner[...] == s for s in range(SEQ)]
    for f in range(SLOTS):
        total = jnp.zeros((ROWS, HEAD), jnp.float32)
        for s in range(SEQ):
            total = jnp.where(owns[s], got[SLOTS * s + f].astype(jnp.float32), total)
        held[f] = total.astype(jnp.bfloat16)
    for send in sends:
        send.start()
    for send in sends:
        send.wait()


def merge(got, owner):
    return pl.pallas_call(
        merge_kernel,
        out_shape=(
            pltpu.HBM((SEQ, SLOTS, ROWS, HEAD), jnp.bfloat16),
            pltpu.HBM((SLOTS, ROWS, HEAD), jnp.bfloat16),
        ),
        in_specs=[whole(), whole(pl.ANY)],
        out_specs=(whole(pltpu.HBM), whole(pltpu.HBM)),
        scratch_shapes=[
            pltpu.VMEM((SLOTS, ROWS, HEAD), jnp.bfloat16),
            pltpu.VMEM((ROWS, 1), jnp.int32),
            pltpu.SemaphoreType.DMA((SEQ + 2,)),
        ],
        compiler_params=pltpu.CompilerParams(vmem_limit_bytes=16 << 20),
        name="merge",
    )(got, in_hbm(owner))


def project_kernel(rows, *refs):
    weights, (kept, sent, matrix, total, own, other, sem) = refs[:SLOTS], refs[SLOTS:]
    loads = [pltpu.make_async_copy(w, matrix.at[j], sem.at[j]) for j, w in enumerate(weights)]
    for load in loads:
        load.start()
    samp = lax.axis_index("samp")
    pair, slot = samp // 8, samp % 8
    slots = [(slot // 2 + step) % 4 * 2 + (slot + cross) % 2 for cross in (0, 1) for step in (0, 1, 3, 2)]
    n = 8 * SEQ
    orders = [
        selection(
            2 * SEQ, n, lambda r: r % SEQ * 8 + 2 * k + jnp.where(pair == 0, r // SEQ, 1 - r // SEQ)
        )
        for k in range(TILES)
    ]
    squares = jnp.zeros((2 * ROWS, 1), jnp.float32)
    for j in range(SLOTS):
        f = slots[j]
        comp = jnp.concatenate([rows[s, f, PROMPT_ROWS:, :] for s in range(SEQ)], axis=0)
        comp = [selected(order, comp).astype(jnp.bfloat16) for order in orders]
        comp = jnp.concatenate(comp, axis=1)
        parts = []
        for r in range(2):
            first = 16 * ((pair + r) % 2)
            for s in range(SEQ):
                tiles = [
                    rows[s, f, pl.ds(pl.multiple_of(32 * k + first, 16), 16), :] for k in range(TILES)
                ]
                parts.append(jnp.concatenate(tiles, axis=1))
            parts.append(comp[SEQ * r : SEQ * r + SEQ])
        block = jnp.concatenate(parts, axis=0)
        wide = block.astype(jnp.float32)
        squares = squares + jnp.sum(wide * wide, axis=1, keepdims=True)
        loads[j].wait()
        product = jnp.dot(block, matrix[j], preferred_element_type=jnp.float32)
        if j == 0:
            total[...] = product
        elif j < SLOTS - 1:
            total[...] += product
        else:
            product = total[...] + product
    high = squares.astype(jnp.bfloat16).astype(jnp.float32)
    lane = lax.broadcasted_iota(jnp.int32, (2 * ROWS, HEAD), 1)
    extra = jnp.where(lane == 0, high, jnp.where(lane == 1, squares - high, 0.0))
    width = product.shape[1]
    for r, out in enumerate((own, other)):
        out[:, :width] = product[ROWS * r : ROWS * r + ROWS].astype(jnp.bfloat16)
        out[:, width:] = extra[ROWS * r : ROWS * r + ROWS].astype(jnp.bfloat16)
    sends = [
        pltpu.make_async_copy(other, sent, sem.at[SLOTS]),
        pltpu.make_async_copy(own, kept, sem.at[SLOTS + 1]),
    ]
    for send in sends:
        send.start()
    for send in sends:
        send.wait()


def project(rows, weights):
    depth, width = weights[0].shape
    shape = (ROWS, width + HEAD)
    return pl.pallas_call(
        project_kernel,
        out_shape=(pltpu.HBM(shape, jnp.bfloat16), pltpu.HBM(shape, jnp.bfloat16)),
        in_specs=[whole()] + [whole(pl.ANY)] * SLOTS,
        out_specs=(whole(pltpu.HBM), whole(pltpu.HBM)),
        scratch_shapes=[
            pltpu.VMEM((SLOTS, depth, width), jnp.bfloat16),
            pltpu.VMEM((2 * ROWS, width), jnp.float32),
            pltpu.VMEM(shape, jnp.bfloat16),
            pltpu.VMEM(shape, jnp.bfloat16),
            pltpu.SemaphoreType.DMA((SLOTS + 2,)),
        ],
        compiler_params=pltpu.CompilerParams(vmem_limit_bytes=28 << 20),
        name="project",
    )(rows, *weights)


def rotate_kernel(kept, given, cos_ref, sin_ref, q_ref, kv_ref, held, mine, sem):
    load = pltpu.make_async_copy(kept, mine, sem.at[SAMP])
    load.start()
    load.wait()
    width = (HEADS + 2) * HEAD
    tail = sum(p[:, width:].astype(jnp.float32) for p in (mine, given))
    squares = tail[:, :1] + tail[:, 1:2]
    inv = lax.rsqrt(squares / FEATURES + NORM_EPS)
    cosine, sine = cos_ref[...], sin_ref[...]
    sends = [pltpu.make_async_copy(held, kv_ref.at[m], sem.at[m]) for m in range(SAMP)]
    for h in (HEADS, HEADS + 1, *range(HEADS)):
        columns = pl.ds(h * HEAD, HEAD)
        u = sum(p[:, columns].astype(jnp.float32) for p in (mine, given)) * inv
        if h <= HEADS:
            u = u * cosine + pltpu.roll(u, HEAD // 2, 1) * sine
        if h < HEADS:
            u = u * LOG2_SCALE
        u = u.astype(jnp.bfloat16)
        if h < HEADS:
            q_ref[pl.ds(h * ROWS, ROWS), :] = u
        else:
            held[:, pl.ds((h - HEADS) * HEAD, HEAD)] = u
        if h == HEADS + 1:
            for send in sends:
                send.start()
    for send in sends:
        send.wait()


def rotate(mine, given, cosine, sine):
    return pl.pallas_call(
        rotate_kernel,
        out_shape=(
            jax.ShapeDtypeStruct((HEADS * ROWS, HEAD), jnp.bfloat16),
            pltpu.HBM((SAMP, ROWS, 2 * HEAD), jnp.bfloat16),
        ),
        in_specs=[whole(pl.ANY)] + [whole()] * 3,
        out_specs=(whole(), whole(pltpu.HBM)),
        scratch_shapes=[
            pltpu.VMEM((ROWS, 2 * HEAD), jnp.bfloat16),
            pltpu.VMEM(mine.shape, jnp.bfloat16),
            pltpu.SemaphoreType.DMA((SAMP + 1,)),
        ],
        compiler_params=pltpu.CompilerParams(vmem_limit_bytes=16 << 20),
        name="rotate",
    )(in_hbm(mine), given, cosine, sine)


def prefix_kernel(count, q_ref, kv_ref, acc_out, stat_out, acc_ref, max_ref, sum_ref, sem, *, slots):
    step = pl.program_id(0)

    @pl.when(step == 0)
    def _():
        acc_ref[...] = jnp.zeros_like(acc_ref)
        max_ref[...] = jnp.full_like(max_ref, MASK_FILL)
        sum_ref[...] = jnp.zeros_like(sum_ref)

    first = step * slots

    def absorb(masked, width):
        keys, values = kv_ref[0, 0, :width, :], kv_ref[1, 0, :width, :]
        values = jnp.concatenate([values, jnp.ones_like(values)], axis=1)
        if masked:
            ids = first + lax.broadcasted_iota(jnp.int32, (1, width), 1)
            bias = jnp.where(ids < count[0], 0.0, MASK_FILL)
        for h in range(HEADS):
            rows = pl.ds(h * ROWS, ROWS)
            scores = lax.dot_general(
                q_ref[rows, :], keys, LAST_DIMS, preferred_element_type=jnp.float32
            )
            if masked:
                scores = scores + bias
            old = max_ref[rows, :]
            new = jnp.maximum(old, jnp.max(scores, axis=1, keepdims=True))
            weights = jnp.exp2(scores - new[:, :1]).astype(jnp.bfloat16)
            factor = jnp.exp2(old - new)
            both = jnp.dot(weights, values, preferred_element_type=jnp.float32)
            acc_ref[rows, :] = acc_ref[rows, :] * factor + both[:, :HEAD]
            sum_ref[rows, :] = sum_ref[rows, :] * factor + both[:, HEAD:]
            max_ref[rows, :] = new

    @pl.when(first + slots <= count[0])
    def _():
        absorb(False, slots)

    @pl.when((first + slots // 2 < count[0]) & (first + slots > count[0]))
    def _():
        absorb(True, slots)

    @pl.when((first < count[0]) & (first + slots // 2 >= count[0]))
    def _():
        absorb(True, slots // 2)

    @pl.when(step == pl.num_programs(0) - 1)
    def _():
        lane = lax.broadcasted_iota(jnp.int32, max_ref.shape, 1)
        max_ref[...] = jnp.where(lane < HEAD // 2, max_ref[...], sum_ref[...])
        sends = [
            pltpu.make_async_copy(acc_ref, acc_out, sem.at[0]),
            pltpu.make_async_copy(max_ref, stat_out, sem.at[1]),
        ]
        for send in sends:
            send.start()
        for send in sends:
            send.wait()


def attend_prefix(count, queries, cache, slots=2048):
    n = queries.shape[0]
    state = pltpu.HBM((n, HEAD), jnp.float32)

    def cache_block(step, count):
        return (0, 0, jnp.minimum(step, lax.div(count[0] - 1, slots)), 0)

    return pl.pallas_call(
        functools.partial(prefix_kernel, slots=slots),
        out_shape=(state, state),
        grid_spec=pltpu.PrefetchScalarGridSpec(
            num_scalar_prefetch=1,
            grid=(cache.shape[2] // slots,),
            in_specs=[
                pl.BlockSpec((n, HEAD), lambda step, count: (0, 0)),
                pl.BlockSpec((2, 1, slots, HEAD), cache_block),
            ],
            out_specs=[whole(pltpu.HBM)] * 2,
            scratch_shapes=[pltpu.VMEM((n, HEAD), jnp.float32)] * 3
            + [pltpu.SemaphoreType.DMA((2,))],
        ),
        compiler_params=pltpu.CompilerParams(
            dimension_semantics=("arbitrary",), vmem_limit_bytes=16 << 20
        ),
        name="prefix",
    )(count, queries, cache)


def finish_kernel(q_ref, acc_in, stat_in, kv, out, block, comp_block, acc_ref, stat_ref, sem):
    loads = [
        pltpu.make_async_copy(acc_in, acc_ref, sem.at[GROUPS]),
        pltpu.make_async_copy(stat_in, stat_ref, sem.at[GROUPS + 1]),
    ]
    for load in loads:
        load.start()
    samp_index = lax.axis_index("samp")
    pair, slot = samp_index // 8, samp_index % 8
    keys = jnp.concatenate([kv[m, :PROMPT_ROWS, :HEAD] for m in range(SAMP)], axis=0)
    values = jnp.concatenate([kv[m, :PROMPT_ROWS, HEAD:] for m in range(SAMP)], axis=0)
    values = jnp.concatenate([values, jnp.ones_like(values)], axis=1)
    comp = jnp.concatenate([kv[slot + 8 * r, PROMPT_ROWS:, :] for r in range(2)], axis=0)
    comp_values = jnp.concatenate([comp[:, HEAD:], jnp.ones_like(comp[:, HEAD:])], axis=1)
    n = keys.shape[0]
    column = lax.broadcasted_iota(jnp.int32, (1, n), 1)
    samp = column // PROMPT_ROWS
    key_id = 256 * (column // 16 % SEQ) + 32 * (samp % 8) + 16 * (samp // 8) + column % 16
    row = lax.broadcasted_iota(jnp.int32, (ROWS, 1), 0)
    own_id = 256 * (row // 16) + 32 * slot + 16 * pair + row % 16
    limit = jnp.where(row < PROMPT_ROWS, own_id, n)
    bias = jnp.where(key_id <= limit, 0.0, MASK_FILL)
    column = lax.broadcasted_iota(jnp.int32, (1, 2 * SEQ), 1)
    live = (column % SEQ == row - PROMPT_ROWS) & (column // SEQ <= pair)
    comp_bias = jnp.where(live, 0.0, MASK_FILL)
    for load in loads:
        load.wait()
    for h in range(HEADS):
        rows = pl.ds(h * ROWS, ROWS)
        q = q_ref[rows, :]
        scores = lax.dot_general(q, keys, LAST_DIMS, preferred_element_type=jnp.float32) + bias
        comp_scores = (
            lax.dot_general(q, comp[:, :HEAD], LAST_DIMS, preferred_element_type=jnp.float32)
            + comp_bias
        )
        old, old_sum = stat_ref[rows, :1], stat_ref[rows, HEAD // 2 : HEAD // 2 + 1]
        new = jnp.maximum(old, jnp.max(scores, axis=1, keepdims=True))
        new = jnp.maximum(new, jnp.max(comp_scores, axis=1, keepdims=True))
        weights = jnp.exp2(scores - new[:, :1]).astype(jnp.bfloat16)
        comp_weights = jnp.exp2(comp_scores - new[:, :1]).astype(jnp.bfloat16)
        factor = jnp.exp2(old - new)
        both = jnp.dot(weights, values, preferred_element_type=jnp.float32)
        both = both + jnp.dot(comp_weights, comp_values, preferred_element_type=jnp.float32)
        context = acc_ref[rows, :] * factor + both[:, :HEAD]
        context = context / (old_sum * factor + both[:, HEAD:])
        for s in range(SEQ):
            block[s, pl.ds(16 * h, 16), :] = context[16 * s : 16 * s + 16].astype(jnp.bfloat16)
            comp_block[s, pl.ds(h, 1), :] = context[PROMPT_ROWS + s : PROMPT_ROWS + s + 1]
    for s in range(SEQ):
        block[s, PROMPT_ROWS:, :] = comp_block[s].astype(jnp.bfloat16)

    def send(g):
        return pltpu.make_async_copy(block, out.at[:, g], sem.at[g])

    for g in range(GROUPS):
        send(g).start()
    for g in range(GROUPS):
        send(g).wait()


def finish(queries, state, kv):
    return pl.pallas_call(
        finish_kernel,
        out_shape=pltpu.HBM((SEQ, GROUPS, ROWS, HEAD), jnp.bfloat16),
        in_specs=[whole(), whole(pl.ANY), whole(pl.ANY), whole()],
        out_specs=whole(pltpu.HBM),
        scratch_shapes=[
            pltpu.VMEM((SEQ, ROWS, HEAD), jnp.bfloat16),
            pltpu.VMEM((SEQ, HEADS, HEAD), jnp.float32),
            pltpu.VMEM(queries.shape, jnp.float32),
            pltpu.VMEM(queries.shape, jnp.float32),
            pltpu.SemaphoreType.DMA((GROUPS + 2,)),
        ],
        compiler_params=pltpu.CompilerParams(vmem_limit_bytes=16 << 20),
        name="finish",
    )(queries, *(in_hbm(block) for block in state), kv)


def products(block, matrix, ready):
    n = GROUPS * HEADS
    order = selection(n, n, lambda r: r % GROUPS * HEADS + r // GROUPS)
    seq = lax.axis_index("seq")
    total = jnp.zeros((ROWS, matrix.shape[2]), jnp.float32)
    for j in range(SEQ):
        first = moved(seq, SHIFTS[j]) * GROUPS
        left = []
        for g in range(GROUPS):
            parts = [block[first + g, pl.ds(16 * h, 16), :] for h in range(HEADS)]
            left.append(jnp.concatenate(parts, axis=1))
        comp = jnp.concatenate([block[first + g, PROMPT_ROWS:, :] for g in range(GROUPS)], axis=0)
        comp = selected(order, comp)
        parts = [comp[GROUPS * h : GROUPS * h + GROUPS] for h in range(HEADS)]
        left.append(jnp.concatenate(parts, axis=1).astype(jnp.bfloat16))
        left = jnp.concatenate(left, axis=0)
        ready(j)
        total = total + jnp.dot(left, matrix[j], preferred_element_type=jnp.float32)
    return total


def near_kernel(same, *refs):
    weights, (total, matrix, sem) = refs[:SEQ], refs[SEQ:]
    loads = [pltpu.make_async_copy(w, matrix.at[j], sem.at[j]) for j, w in enumerate(weights)]
    for load in loads:
        load.start()
    total[...] = products(same, matrix, lambda j: loads[j].wait())


def near_output(same, weights):
    depth, width = weights[0].shape
    return pl.pallas_call(
        near_kernel,
        out_shape=(
            jax.ShapeDtypeStruct((ROWS, width), jnp.float32),
            pltpu.VMEM((SEQ, depth, width), jnp.bfloat16),
        ),
        in_specs=[whole()] + [whole(pl.ANY)] * SEQ,
        out_specs=(whole(), whole()),
        scratch_shapes=[pltpu.SemaphoreType.DMA((SEQ,))],
        compiler_params=pltpu.CompilerParams(vmem_limit_bytes=18 << 20),
        name="near_output",
    )(same, *weights)


def far_kernel(rest, crossed, near, matrix, prompt_out, comp_out):
    core = lax.axis_index("samp") % 2
    totals = (near[...], products(crossed, matrix, lambda j: None))
    for r in range(2):
        for g in range(GROUPS):
            slot = 2 * (g % 4) + (core + r) % 2
            at = pl.multiple_of(32 * slot + 16 * (g // 4), 16)
            parts = [
                rest[slot, pl.ds(32 * k + 16 * (g // 4), 16), :].astype(jnp.float32)
                for k in range(TILES)
            ]
            prompt_out[pl.ds(at, 16), :] = (
                totals[r][16 * g : 16 * g + 16] + jnp.concatenate(parts, axis=1)
            ).astype(jnp.bfloat16)
    comp = jnp.concatenate([rest[f, PROMPT_ROWS:, :] for f in range(SLOTS)], axis=0)

    def rest_of(r, k):
        slot = 2 * (r % 4) + (r // GROUPS + core) % 2
        return slot * 8 + 2 * k + r % GROUPS // 4

    parts = [
        selected(selection(SAMP, 8 * SLOTS, lambda r: rest_of(r, k)), comp) for k in range(TILES)
    ]
    last = jnp.concatenate([t[PROMPT_ROWS:] for t in totals], axis=0)
    last = (last + jnp.concatenate(parts, axis=1)).astype(jnp.bfloat16)
    order = selection(
        SAMP, SAMP, lambda r: (r // 2 + core) % 2 * GROUPS + r % 2 * 4 + r // 4
    )
    comp_out[...] = selected(order, last).astype(jnp.bfloat16).reshape(comp_out.shape)


def far_output(rest, crossed, near, matrix):
    width = near.shape[1]
    return pl.pallas_call(
        far_kernel,
        out_shape=(
            jax.ShapeDtypeStruct((2 * PROMPT_ROWS, width), jnp.bfloat16),
            jax.ShapeDtypeStruct((SAMP // 2, 2, width), jnp.bfloat16),
        ),
        in_specs=[whole()] * 4,
        out_specs=(whole(), whole()),
        compiler_params=pltpu.CompilerParams(vmem_limit_bytes=22 << 20),
        name="far_output",
    )(rest, crossed, near, matrix)


def body(
    prompt_ids,
    comp_ids,
    prefix_len,
    prompt_offset,
    embed_table,
    attn_gain,
    query_key_value_weight,
    w_out,
    key_value_cache,
):
    seq_index = lax.axis_index("seq")
    samp_index = lax.axis_index("samp")
    pair, slot = samp_index // 8, samp_index % 8
    vocab_rows, width = embed_table.shape

    scaled = query_key_value_weight.astype(jnp.float32) * attn_gain.astype(jnp.float32)[:, None]
    scaled = scaled.astype(jnp.bfloat16)
    out_flip = to_seq(w_out, (0, 1))
    w_next, w_last = to_seq(w_out, (3, 0)), to_seq(w_out, (1, 0))
    scaled_next, scaled_last = to_ring(scaled, 3), to_ring(scaled, 1)

    ids = jnp.concatenate([prompt_ids, comp_ids.reshape(-1)])
    local = jnp.clip(ids - seq_index * vocab_rows, 0, vocab_rows - 1)
    picked = embed_table.at[local].get(mode="promise_in_bounds")
    pieces = arrange(picked.reshape(-1, 32, width))
    got = exchange(pieces, ("seq", "samp"), SEQ_SLOT)
    piece_at = SLOTS * seq_index + slot
    own_prompt_ids = lax.dynamic_slice_in_dim(prompt_ids, 32 * piece_at, 32, 0)
    own_comp_ids = lax.dynamic_slice_in_dim(comp_ids.reshape(-1), 2 * piece_at, 2, 0)
    own_ids = jnp.concatenate([jnp.tile(own_prompt_ids, TILES), jnp.tile(own_comp_ids, TILES)])
    owner = (own_ids // vocab_rows)[:, None]
    copies, merged = merge(got, owner)

    rows = exchange(copies, "seq")
    by_ring, _ = lax.optimization_barrier((scaled, copies))
    scaled_far = to_ring(by_ring, 2)
    scales = [scaled, scaled_next, scaled_last, scaled_far]
    scales = scales + [to_other_core(w) for w in scales]
    w_flip, w_last, _ = lax.optimization_barrier((out_flip, w_last, scaled_far))
    w_next_flip, w_last_flip = to_seq(w_flip, (3, 0)), to_seq(w_flip, (1, 0))
    w_far = to_seq(w_last, (1, 0))

    mine, sent = project(rows, scales)
    given = to_other_pair(sent)
    rest = exchange(merged, "samp", SAME_PAIR)
    given, rest = lax.optimization_barrier((given, rest))

    row = jnp.arange(ROWS, dtype=jnp.int32)
    own_prompt = 256 * (row // 16) + 32 * slot + 16 * pair + row % 16
    position = jnp.where(row < PROMPT_ROWS, own_prompt, 2048 + pair) + prompt_offset[0]
    angles = position.astype(jnp.float32)[:, None] * rope_freqs(HEAD)[None, :]
    cosine, sine = jnp.cos(angles), jnp.sin(angles)
    cosine = jnp.concatenate([cosine, cosine], axis=1)
    sine = jnp.concatenate([-sine, sine], axis=1)
    queries, kv = rotate(mine, given, cosine, sine)
    all_kv = exchange(kv, "samp")
    queries, w_next_flip = lax.optimization_barrier((queries, w_next_flip))
    w_far_flip = to_seq(w_next_flip, (3, 0))
    state = attend_prefix(
        prefix_len, queries, pltpu.with_memory_space_constraint(key_value_cache, pltpu.HBM)
    )
    weights = [w_out, w_flip, w_next, w_next_flip, w_last, w_last_flip, w_far, w_far_flip]
    context = finish(queries, state, all_kv)
    context = context.reshape(SEQ * GROUPS, ROWS, HEAD)

    same = exchange(context, ("seq", "samp"), SEQ_GROUP)
    crossed = to_other_core(same)
    near, matrix = near_output(same, weights)
    prompt_out, comp_out = far_output(rest, crossed, near, matrix)
    return prompt_out, comp_out


def solution(mesh):
    placed = (
        P(),
        P(),
        P(),
        P(),
        P("seq", "samp"),
        P("samp"),
        P("samp", "seq"),
        P("seq", "samp"),
        P(None, "seq", None, None),
    )
    return jax.shard_map(
        body,
        mesh=mesh,
        in_specs=placed,
        out_specs=(P("seq", "samp"), P("seq", None, "samp")),
        check_vma=False,
    )
```
